128 devices in a mesh: row: 16 (over y, x), col: 8 (over z, core).
Axes of the slice: x: 4, y: 4, z: 4, core: 2. Of those that a mesh axis runs over, the one named last changes fastest.
Arguments:
- hidden_in: bfloat16 [4096, 7168], P('row'), may hold values from -6 to 6
- norm_gain: float32 [7168], replicated, may hold values from 0.5 to 1.5
- norm_bias: float32 [7168], replicated, may hold values from -3 to 3
- w_query: bfloat16 [7168, 6144], P('row', 'col'), may hold values from -0.0625 to 0.0625
- w_keyval: bfloat16 [7168, 2, 6144], P('row', None, 'col'), may hold values from -0.125 to 0.125
- bias_query: float32 [6144], P('col'), may hold values from -3 to 3
- bias_keyval: float32 [2, 6144], P(None, 'col'), may hold values from -3 to 3
- cache_keys: bfloat16 [16, 4096, 6144], P('row', None, 'col'), may hold values from -60 to 60
- cache_values: bfloat16 [16, 4096, 6144], P('row', None, 'col'), may hold values from -12 to 12
- cache_lengths: int32 [16], replicated, may hold values from 2 to 4096
- owner_slot: int32 [16], replicated, may hold values from 0 to 15, each once
- w_out: bfloat16 [6144, 7168], P('col', 'row'), may hold values from -0.3125 to 0.3125
- bias_out: float32 [7168], P('col'), may hold values from -3 to 3
Outputs:
- hidden_out: bfloat16 [4096, 7168], P('row', 'col')
- new_keys: bfloat16 [16, 256, 6144], P('row', None, 'col')
- new_values: bfloat16 [16, 256, 6144], P('row', None, 'col')
The draws below stay inside these ranges and needn't reach their ends.
Inputs may be any that keep to these rules, and one draw needn't show every extreme that they name: `owner_slot`: each slot is the owner of exactly one request.
All inputs are finite; a program needn't handle non-finite values.
Results may differ from the reference program's by a relative error of at most 0.01375.
Values may be sent and summed in bfloat16 or wider, within the bound.
A program may use at most 192 MiB of HBM per device.

```python
import jax
import jax.numpy as jnp
from jax import lax

D = 7168
HEADS = 48
HEAD = 128
GROUP = 256
CACHE = 4096
HD = 6144
REQS = 16
TOKENS = 4096


def draw_cache_lengths(key, part):
    key_one, key_two, key_three, key_four = jax.random.split(jax.random.fold_in(key, 11), 4)
    first_draw = jax.random.randint(key_one, (REQS,), 2, CACHE + 1)
    second_draw = jax.random.randint(key_two, (REQS,), 2, CACHE + 1)
    lengths = jnp.minimum(first_draw, second_draw)
    longest = jax.random.randint(key_three, (), 0, REQS)
    shortest = (longest + jax.random.randint(key_four, (), 1, REQS)) % REQS
    slot_ids = jnp.arange(REQS)
    lengths = jnp.where(slot_ids == longest, CACHE, jnp.where(slot_ids == shortest, 2, lengths))
    return lengths.astype(jnp.int32)


def draw_cache_keys(key, part):
    key_one = jax.random.fold_in(jax.random.fold_in(key, 23), 0)
    result = jnp.clip(2.0 * jax.random.normal(key_one, (REQS, CACHE, HD), jnp.float32), -12.0, 12.0)
    return result.astype(jnp.bfloat16)


def steps_of(own_key, dims, pieces, least, top_value):
    def one(axis_at, shards_of):
        heights = jax.random.uniform(jax.random.fold_in(jax.random.fold_in(own_key, 6), axis_at), (shards_of,), jnp.float32, least / len(pieces), top_value / len(pieces))
        return jnp.repeat(jnp.exp(heights), dims[axis_at] // shards_of).reshape((-1,) + (1,) * (len(dims) - axis_at - 1))

    factor_of = one(*pieces[0])
    for cut in pieces[1:]:
        factor_of = factor_of * one(*cut)
    return factor_of


def noise(key, shape, deviation, bound, cuts=(), held_as=jnp.bfloat16):
    values = deviation * jax.random.normal(key, shape, jnp.float32)
    if cuts:
        values = values * steps_of(key, shape, cuts, -0.22, 0.18)
    return jnp.clip(values, -bound, bound).astype(held_as)


def setup_inputs(seed: int = 0) -> dict:
    arg_keys = jax.random.split(jax.random.key(seed), 14)
    return {
        "hidden_in": noise(arg_keys[0], (TOKENS, D), 1.0, 6.0, ((0, 16),)),
        "norm_gain": jnp.clip(1.0 + 0.1 * jax.random.normal(arg_keys[1], (D,), jnp.float32), 0.5, 1.5),
        "norm_bias": noise(arg_keys[2], (D,), 0.5, 3.0, (), jnp.float32),
        "w_query": noise(arg_keys[3], (D, HD), D ** -0.5, 0.0625, ((0, 16), (1, 8))),
        "w_keyval": noise(arg_keys[4], (D, 2, HD), (D // 4) ** -0.5, 0.125, ((0, 16), (2, 8))),
        "bias_query": noise(arg_keys[5], (HD,), 0.5, 3.0, ((0, 8),), jnp.float32),
        "bias_keyval": noise(arg_keys[6], (2, HD), 0.5, 3.0, ((1, 8),), jnp.float32),
        "cache_keys": draw_cache_keys(jax.random.fold_in(arg_keys[13], 71), 0),
        "cache_values": noise(arg_keys[8], (REQS, CACHE, HD), 2.0, 12.0, ((0, 16), (2, 8))),
        "cache_lengths": draw_cache_lengths(jax.random.fold_in(arg_keys[13], 71), 0),
        "owner_slot": jax.random.permutation(arg_keys[10], REQS).astype(jnp.int32),
        "w_out": noise(arg_keys[11], (HD, D), (HD // 16) ** -0.5, 0.3125, ((0, 8), (1, 16))),
        "bias_out": noise(arg_keys[12], (D,), 0.5, 3.0, ((0, 8),), jnp.float32),
    }


def normalize(inputs, gain, bias):
    row_mean = lax.optimization_barrier(jnp.mean(inputs, axis=-1, keepdims=True))
    centered = inputs - row_mean
    row_var = lax.optimization_barrier(jnp.mean(centered * centered, axis=-1, keepdims=True))
    return centered * lax.rsqrt(row_var + 1e-05) * gain + bias

def reference(hidden_in, norm_gain, norm_bias, w_query, w_keyval, bias_query, bias_keyval, cache_keys, cache_values, cache_lengths, owner_slot, w_out, bias_out):
    inputs = hidden_in.astype(jnp.float32)
    normed = normalize(inputs, norm_gain, norm_bias).astype(jnp.bfloat16)
    q_scale = HEAD ** (-0.5)
    query_all = ((jnp.dot(normed, w_query, preferred_element_type=jnp.float32) + bias_query) * q_scale).astype(jnp.bfloat16)
    keyval = (jnp.dot(normed, w_keyval.reshape(D, 2 * HD), preferred_element_type=jnp.float32) + bias_keyval.reshape(2 * HD)).astype(jnp.bfloat16)
    keys_all = keyval[:, :HD]
    values_all = keyval[:, HD:]
    slot_ids = jnp.arange(REQS, dtype=jnp.int32)
    is_owner = owner_slot[:, None] == slot_ids[None, :]
    inverse = lax.optimization_barrier(jnp.sum(jnp.where(is_owner, slot_ids[:, None], 0), axis=0)).astype(jnp.int32)

    def per_slot(slot):
        request = inverse[slot]
        first_row = (request * GROUP).astype(jnp.int32)
        query_rows = lax.dynamic_slice_in_dim(query_all, first_row, GROUP, 0).reshape(GROUP, HEADS, HEAD).astype(jnp.float32)
        new_k = lax.dynamic_slice_in_dim(keys_all, first_row, GROUP, 0)
        new_v = lax.dynamic_slice_in_dim(values_all, first_row, GROUP, 0)
        key_rows = jnp.concatenate([cache_keys[slot], new_k], axis=0).reshape(CACHE + GROUP, HEADS, HEAD).astype(jnp.float32)
        value_rows = jnp.concatenate([cache_values[slot], new_v], axis=0).reshape(CACHE + GROUP, HEADS, HEAD).astype(jnp.float32)
        length = cache_lengths[request]
        positions = jnp.arange(CACHE + GROUP, dtype=jnp.int32)[None, :]
        query_pos = jnp.arange(GROUP, dtype=jnp.int32)[:, None]
        is_valid = jnp.where(positions < CACHE, positions < length, positions - CACHE <= query_pos)
        scores = jnp.einsum('qhd,khd->hqk', query_rows, key_rows)
        masked = jnp.where(is_valid[None], scores, -jnp.inf)
        row_max = lax.optimization_barrier(jnp.max(masked, axis=-1))
        probs = jnp.where(is_valid[None], jnp.exp(scores - row_max[..., None]), 0.0)
        total = lax.optimization_barrier(jnp.sum(probs, axis=-1))
        rounded = probs.astype(jnp.bfloat16).astype(jnp.float32)
        attended = jnp.einsum('hqk,khd->hqd', rounded, value_rows) / total[..., None]
        return attended.transpose(1, 0, 2).reshape(GROUP, HD).astype(jnp.bfloat16)
    attended_all = lax.map(per_slot, slot_ids)
    new_keys = jnp.take(keys_all.reshape(REQS, GROUP, HD), inverse, axis=0)
    new_values = jnp.take(values_all.reshape(REQS, GROUP, HD), inverse, axis=0)
    ordered = jnp.take(attended_all, owner_slot, axis=0).reshape(TOKENS, HD)
    projected = jnp.dot(ordered, w_out, preferred_element_type=jnp.float32)
    hidden_out = (projected + bias_out + inputs).astype(jnp.bfloat16)
    return (hidden_out, new_keys, new_values)
```

```python
import functools

import jax
import jax.numpy as jnp
from jax import lax
from jax.experimental import pallas as pl
from jax.experimental.pallas import tpu as pltpu
from jax.sharding import PartitionSpec as P

HEAD = 128
MESH = pl.DeviceIdType.MESH
BF16 = jnp.bfloat16
F32 = jnp.float32
NEG = -1e30


def place():
    row, col = lax.axis_index("row"), lax.axis_index("col")
    return row, col, lax.div(row, 4), lax.rem(row, 4), lax.div(col, 2), lax.rem(col, 2)


def send(src, dst, send_sem, recv_sem, row, col):
    copy = pltpu.make_async_remote_copy(
        src_ref=src,
        dst_ref=dst,
        send_sem=send_sem,
        recv_sem=recv_sem,
        device_id=(row, col),
        device_id_type=MESH,
    )
    copy.start()
    return copy


def greet(peers):
    barrier = pltpu.get_barrier_semaphore()
    for row, col in peers:
        pl.semaphore_signal(barrier, inc=1, device_id=(row, col), device_id_type=MESH)
    pl.semaphore_wait(barrier, len(peers))


class Ring:
    def __init__(self, me, device, block, half, send_sem, recv_sem):
        self.me, self.device, self.block, self.half = me, device, block, half
        self.send_sem, self.recv_sem = send_sem, recv_sem
        self.copies = []

    def start(self):
        for i, step in enumerate((1, 3)):
            to = self.device(lax.rem(self.me + step, 4))
            view = self.block(self.me)
            self.copies.append(send(view, view, self.send_sem(i), self.recv_sem(i), *to))

    def forward(self):
        for i, step in enumerate((1, 3)):
            self.copies[i].wait_recv()
            to = self.device(lax.rem(self.me + step, 4))
            view = self.half(lax.rem(self.me + 4 - step, 4), i)
            self.copies.append(send(view, view, self.send_sem(2 + i), self.recv_sem(2 + i), *to))

    def finish(self):
        for copy in self.copies[2:]:
            copy.wait_recv()

    def drain(self):
        for copy in self.copies:
            copy.wait_send()


def qkv_kernel(
    inv_ref, act_ref, wq_ref, wkv_ref, bias_ref, q_ref, k_ref, v_ref,
    ybuf, abuf, wbuf, psend, rbuf, acc,
    lsem, xs, xr, ys, yr, zs, zr, cs, cr, ws, wr, ps, pr,
):
    row, col, y, x, z, core = place()
    at = lambda yy, xx: yy * 4 + xx
    other = z * 2 + (1 - core)
    peers = [(at(y, lax.rem(x + d, 4)), col) for d in (1, 2, 3)]
    peers += [(at(lax.rem(y + d, 4), x), col) for d in (1, 3)]
    peers += [(row, lax.rem(z + d, 4) * 2 + core) for d in (1, 3)]
    peers += [(row, other)]

    local = [pltpu.make_async_copy(act_ref.at[x], ybuf.at[y, x], lsem.at[0])]
    local += [pltpu.make_async_copy(wq_ref, wbuf.at[0, y], lsem.at[1])]
    local += [pltpu.make_async_copy(wkv_ref.at[i], wbuf.at[1 + i, y], lsem.at[2 + i]) for i in (0, 1)]
    for copy in local:
        copy.start()
    greet(peers)

    xcopies = []
    for d in (1, 2, 3):
        to = lax.rem(x + d, 4)
        xcopies.append(
            send(act_ref.at[to], ybuf.at[y, x], xs.at[d - 1], xr.at[d - 1], at(y, to), col)
        )
    local[0].wait()
    for copy in xcopies:
        copy.wait_recv()
    yring = Ring(
        y,
        lambda o: (at(o, x), col),
        lambda o: ybuf.at[o],
        lambda o, i: ybuf.at[o, pl.ds(2 * i, 2)],
        lambda i: ys.at[i],
        lambda i: yr.at[i],
    )
    yring.start()
    yring.forward()
    wring = [
        Ring(
            y,
            lambda o: (at(o, x), col),
            lambda o, j=j: wbuf.at[j, o],
            lambda o, i, j=j: wbuf.at[j, o, pl.ds(224 * i, 224)],
            lambda i, j=j: ws.at[j, i],
            lambda i, j=j: wr.at[j, i],
        )
        for j in range(3)
    ]
    for copy in local[1:]:
        copy.wait()
    wring[0].start()
    yring.finish()
    for s in range(4):
        request = inv_ref[y * 4 + s]
        abuf[s, col] = ybuf[lax.div(request, 4), lax.rem(request, 4)]
    zring = Ring(
        z,
        lambda o: (row, o * 2 + core),
        lambda o: abuf.at[:, o * 2 + core],
        lambda o, i: abuf.at[pl.ds(2 * i, 2), o * 2 + core],
        lambda i: zs.at[i],
        lambda i: zr.at[i],
    )
    zring.start()
    ccopies = []

    def across(view):
        i = len(ccopies)
        ccopies.append(send(view, view, cs.at[i], cr.at[i], row, other))

    across(zring.block(z))
    zring.forward()
    across(zring.block(lax.rem(z + 3, 4)))
    across(zring.block(lax.rem(z + 1, 4)))
    wring[0].forward()
    wring[1].start()
    zring.finish()
    across(zring.block(lax.rem(z + 2, 4)))
    for copy in ccopies:
        copy.wait_recv()

    def multiply(part):
        wring[part].finish()

        def block(i, carry):
            to = lax.rem(x + i + 1, 4)
            rows = abuf[to].reshape(256, 1792)
            for n in range(3):
                cols = pl.ds(n * 256, 256)
                out = jnp.dot(
                    rows,
                    wbuf[part, :, :, cols].reshape(1792, 256),
                    preferred_element_type=F32,
                )
                acc[part, :, cols] = out
                psend[part, i, :, cols] = out.astype(BF16)

            @pl.when(i < 3)
            def _():
                send(
                    psend.at[part, i], rbuf.at[part, i], ps.at[part, i], pr.at[part, i],
                    at(y, to), col,
                )

            return carry

        lax.fori_loop(0, 4, block, 0)

    def arrived(part, i):
        return pltpu.make_async_remote_copy(
            src_ref=psend.at[part, i],
            dst_ref=rbuf.at[part, i],
            send_sem=ps.at[part, i],
            recv_sem=pr.at[part, i],
            device_id=(at(y, lax.rem(x + i + 1, 4)), col),
            device_id_type=MESH,
        )

    def total(part):
        for i in range(3):
            arrived(part, i).wait_recv()
        out = acc[part]
        for i in range(3):
            out = out + rbuf[part, i].astype(F32)
        return out + bias_ref[part][None, :]

    multiply(0)
    wring[1].forward()
    wring[2].start()
    multiply(1)
    q_ref[...] = (total(0) * (HEAD**-0.5)).astype(BF16)
    wring[2].forward()
    k_ref[...] = total(1).astype(BF16)
    multiply(2)
    v_ref[...] = total(2).astype(BF16)

    for copy in xcopies + ccopies:
        copy.wait_send()
    for ring in [yring, zring] + wring:
        ring.drain()
    for part in range(3):
        for i in range(3):
            arrived(part, i).wait_send()


def project(inverse, act, wq, wkv, bias):
    dma = pltpu.SemaphoreType.DMA
    vmem = pl.BlockSpec(memory_space=pltpu.VMEM)
    out = jax.ShapeDtypeStruct((256, 768), BF16)
    return pl.pallas_call(
        qkv_kernel,
        out_shape=(out, out, out),
        in_specs=[pl.BlockSpec(memory_space=pltpu.SMEM), vmem]
        + [pl.BlockSpec(memory_space=pl.ANY)] * 2 + [vmem],
        out_specs=(vmem, vmem, vmem),
        scratch_shapes=[
            pltpu.VMEM((4, 4, 32, 1792), BF16),
            pltpu.VMEM((4, 8, 32, 1792), BF16),
            pltpu.VMEM((3, 4, 448, 768), BF16),
            pltpu.VMEM((3, 4, 256, 768), BF16),
            pltpu.VMEM((3, 3, 256, 768), BF16),
            pltpu.VMEM((3, 256, 768), F32),
            dma((4,)),
            dma((3,)), dma((3,)),
            dma((4,)), dma((4,)),
            dma((4,)), dma((4,)),
            dma((4,)), dma((4,)),
            dma((3, 4)), dma((3, 4)),
            dma((3, 3)), dma((3, 3)),
        ],
        compiler_params=pltpu.CompilerParams(
            collective_id=0, has_side_effects=True, vmem_limit_bytes=56 * 2**20
        ),
        name="qkv",
    )(inverse, act, wq, wkv, bias)


KEYS = 512


def flash_kernel(len_ref, q_ref, ck_ref, cv_ref, nk_ref, nv_ref, out_ref, m_s, l_s, o_s):
    step = pl.program_id(0)
    heads = q_ref.shape[1] // HEAD

    @pl.when(step == 0)
    def _():
        m_s[...] = jnp.full_like(m_s, NEG)
        l_s[...] = jnp.zeros_like(l_s)
        o_s[...] = jnp.zeros_like(o_s)

    def visit(keys, values, bias):
        for h in range(heads):
            lanes = slice(h * HEAD, (h + 1) * HEAD)
            scores = lax.dot_general(
                q_ref[:, lanes], keys[:, lanes], (((1,), (1,)), ((), ())),
                preferred_element_type=F32,
            )
            scores = scores + bias
            old = m_s[h]
            new = jnp.maximum(old, jnp.max(scores, axis=1, keepdims=True))
            probs = jnp.exp(scores - new)
            factor = jnp.exp(old - new)
            m_s[h] = new
            l_s[h] = l_s[h] * factor + jnp.sum(probs, axis=1, keepdims=True)
            o_s[h] = o_s[h] * factor + jnp.dot(
                probs.astype(BF16), values[:, lanes], preferred_element_type=F32
            )

    @pl.when(step * KEYS < len_ref[0])
    def _():
        pos = step * KEYS + lax.broadcasted_iota(jnp.int32, (1, KEYS), 1)
        visit(ck_ref[0], cv_ref[0], jnp.where(pos < len_ref[0], 0.0, NEG))

    @pl.when(step == pl.num_programs(0) - 1)
    def _():
        shape = (nk_ref.shape[0], nk_ref.shape[0])
        late = lax.broadcasted_iota(jnp.int32, shape, 1) > lax.broadcasted_iota(jnp.int32, shape, 0)
        visit(nk_ref[...], nv_ref[...], jnp.where(late, NEG, 0.0))
        for h in range(heads):
            out_ref[:, h * HEAD : (h + 1) * HEAD] = (o_s[h] / l_s[h]).astype(BF16)


def attend(length, query, cache_k, cache_v, new_k, new_v):
    rows, width = query.shape
    heads = width // HEAD
    steps = cache_k.shape[1] // KEYS
    whole = pl.BlockSpec((rows, width), lambda i, n: (0, 0))
    cache = pl.BlockSpec((1, KEYS, width), lambda i, n: (0, i, 0))
    return pl.pallas_call(
        flash_kernel,
        out_shape=jax.ShapeDtypeStruct((rows, width), BF16),
        grid_spec=pltpu.PrefetchScalarGridSpec(
            num_scalar_prefetch=1,
            grid=(steps,),
            in_specs=[whole, cache, cache, whole, whole],
            out_specs=whole,
            scratch_shapes=[
                pltpu.VMEM((heads, rows, 1), F32),
                pltpu.VMEM((heads, rows, 1), F32),
                pltpu.VMEM((heads, rows, HEAD), F32),
            ],
        ),
        compiler_params=pltpu.CompilerParams(vmem_limit_bytes=48 * 2**20),
        name="flash",
    )(length, query, cache_k, cache_v, new_k, new_v)


def out_kernel(
    own_ref, att_ref, w_ref, out_ref,
    ag0, ag1, csend, crecv, mine, zsend, zrecv, fsend, frecv,
    lsem, as_, ar, bs, br, cs, cr, zs, zr, fs, fr,
):
    row, col, y, x, z, core = place()
    at = lambda yy, xx: yy * 4 + xx
    other = z * 2 + (1 - core)
    peers = [(at(y, lax.rem(x + d, 4)), col) for d in (1, 3)]
    peers += [(at(lax.rem(y + d, 4), x), col) for d in (1, 3)]
    peers += [(row, lax.rem(z + d, 4) * 2 + core) for d in (1, 2, 3)]
    peers += [(row, other)]
    targets = [(2 * col + i, lax.div(row, 2)) for i in (0, 1)]
    barrier = pltpu.get_barrier_semaphore()
    selves = [jnp.logical_and(t[0] == row, t[1] == col) for t in targets]

    ag = (ag0, ag1)
    local = []
    for t in range(2):
        for h in range(2):
            local.append(
                pltpu.make_async_copy(
                    att_ref.at[pl.ds(t * 128 + h * 64, 64)], ag[t].at[h, y, x], lsem.at[t, h]
                )
            )
            local[-1].start()
    for r, c in peers:
        pl.semaphore_signal(barrier, inc=1, device_id=(r, c), device_id_type=MESH)
    for i in range(2):

        @pl.when(jnp.logical_not(selves[i]))
        def _():
            pl.semaphore_signal(barrier, inc=1, device_id=targets[i], device_id_type=MESH)

    alone = (lax.div(row, 2) == col).astype(jnp.int32)
    pl.semaphore_wait(barrier, len(peers) + 2 - alone)

    for copy in local:
        copy.wait()

    def xline(o):
        return (at(y, o), col)

    def yline(o):
        return (at(o, x), col)

    first, second = [], []
    for t in range(2):
        sem = lambda s, p, t=t: (lambda i: s.at[t, p, i])
        first.append((
            Ring(x, xline, lambda o, t=t: ag[t].at[0, y, o],
                 lambda o, i, t=t: ag[t].at[0, y, o, pl.ds(32 * i, 32)], sem(as_, 0), sem(ar, 0)),
            Ring(y, yline, lambda o, t=t: ag[t].at[1, o, x],
                 lambda o, i, t=t: ag[t].at[1, o, x, pl.ds(32 * i, 32)], sem(bs, 0), sem(br, 0)),
        ))
        second.append((
            Ring(y, yline, lambda o, t=t: ag[t].at[0, o],
                 lambda o, i, t=t: ag[t].at[0, o, pl.ds(2 * i, 2)], sem(as_, 1), sem(ar, 1)),
            Ring(x, xline, lambda o, t=t: ag[t].at[1, :, o],
                 lambda o, i, t=t: ag[t].at[1, pl.ds(2 * i, 2), o], sem(bs, 1), sem(br, 1)),
        ))

    def each(rings, what):
        for ring in rings:
            getattr(ring, what)()

    each(first[0], "start")
    each(first[0], "forward")
    each(first[1], "start")
    each(first[0], "finish")
    each(second[0], "start")
    each(first[1], "forward")
    each(first[1], "finish")
    each(second[0], "forward")
    each(second[1], "start")

    def partial(t, g, to_core):
        rows = []
        for j in range(4):
            owner = own_ref[g * 8 + j // 2 * 4 + to_core * 2 + j % 2]
            oy, ox = lax.div(owner, 4), lax.rem(owner, 4)
            rows += [ag[t][0, oy, ox], ag[t][1, oy, ox]]
        out = jnp.dot(jnp.concatenate(rows, axis=0), w_ref[...], preferred_element_type=F32)
        return out.reshape(4, 128, 448)

    copies = []

    def reduce(t):
        def away(g, carry):
            csend[t, pl.ds(g * 4, 4)] = partial(t, g, 1 - core).astype(BF16)
            return carry

        lax.fori_loop(0, 2, away, 0)
        ccopy = send(csend.at[t], crecv.at[t], cs.at[t], cr.at[t], row, other)

        def stay(g, carry):
            mine[t, pl.ds(g * 4, 4)] = partial(t, g, core)
            return carry

        lax.fori_loop(0, 2, stay, 0)
        ccopy.wait_recv()
        copies.append(ccopy)
        zcopies = []
        for d in (1, 2, 3):
            to = lax.rem(z + d, 4)
            for i in range(2):
                zsend[t, d - 1, i] = (
                    mine[t, to * 2 + i] + crecv[t, to * 2 + i].astype(F32)
                ).astype(BF16)
            zcopies.append(
                send(zsend.at[t, d - 1], zrecv.at[t, d - 1], zs.at[t, d - 1], zr.at[t, d - 1],
                     row, to * 2 + core)
            )
        copies.extend(zcopies)
        return zcopies

    def hand_over(t, zcopies):
        for copy in zcopies:
            copy.wait_recv()
        for i in range(2):
            total = mine[t, z * 2 + i] + crecv[t, z * 2 + i].astype(F32)
            for d in range(3):
                total = total + zrecv[t, d, i].astype(F32)
            fsend[t, i] = total.astype(BF16)

            @pl.when(jnp.logical_not(selves[i]))
            def _():
                last(t, i).start()

            @pl.when(selves[i])
            def _():
                frecv[t, lax.rem(row, 2)] = fsend[t, i]

    def last(t, i):
        return pltpu.make_async_remote_copy(
            src_ref=fsend.at[t, i],
            dst_ref=frecv.at[t, lax.rem(row, 2)],
            send_sem=fs.at[t, i],
            recv_sem=fr.at[t, lax.rem(row, 2)],
            device_id=targets[i],
            device_id_type=MESH,
        )

    each(second[0], "finish")
    z0 = reduce(0)
    each(second[1], "forward")
    hand_over(0, z0)
    each(second[1], "finish")
    z1 = reduce(1)
    hand_over(1, z1)

    for t in range(2):
        for k in range(2):

            @pl.when(jnp.logical_not(selves[k]))
            def _():
                pltpu.make_async_remote_copy(
                    src_ref=fsend.at[t, k], dst_ref=frecv.at[t, k], send_sem=fs.at[t, k],
                    recv_sem=fr.at[t, k], device_id=targets[k], device_id_type=MESH,
                ).wait_recv()

            out_ref[k, pl.ds(t * 128, 128)] = frecv[t, k]
    for t in range(2):
        for i in range(2):

            @pl.when(jnp.logical_not(selves[i]))
            def _():
                last(t, i).wait_send()

    for copy in copies:
        copy.wait_send()
    for pair in first + second:
        each(pair, "drain")


def combine(owner_slot, attended, w_out):
    dma = pltpu.SemaphoreType.DMA
    vmem = pl.BlockSpec(memory_space=pltpu.VMEM)
    return pl.pallas_call(
        out_kernel,
        out_shape=jax.ShapeDtypeStruct((2, 256, 448), BF16),
        in_specs=[pl.BlockSpec(memory_space=pltpu.SMEM), vmem, vmem],
        out_specs=vmem,
        scratch_shapes=[
            pltpu.VMEM((2, 4, 4, 64, 768), BF16),
            pltpu.VMEM((2, 4, 4, 64, 768), BF16),
            pltpu.VMEM((2, 8, 128, 448), BF16),
            pltpu.VMEM((2, 8, 128, 448), BF16),
            pltpu.VMEM((2, 8, 128, 448), F32),
            pltpu.VMEM((2, 3, 2, 128, 448), BF16),
            pltpu.VMEM((2, 3, 2, 128, 448), BF16),
            pltpu.VMEM((2, 2, 128, 448), BF16),
            pltpu.VMEM((2, 2, 128, 448), BF16),
            dma((2, 2)),
            dma((2, 2, 4)), dma((2, 2, 4)),
            dma((2, 2, 4)), dma((2, 2, 4)),
            dma((2,)), dma((2,)),
            dma((2, 3)), dma((2, 3)),
            dma((2, 2)), dma((2, 2)),
        ],
        compiler_params=pltpu.CompilerParams(
            collective_id=1, has_side_effects=True, vmem_limit_bytes=56 * 2**20
        ),
        name="out",
    )(owner_slot, attended, w_out)


def normalize(inputs, gain, bias):
    row_mean = jnp.mean(inputs, axis=-1, keepdims=True)
    centered = inputs - row_mean
    row_var = jnp.mean(centered * centered, axis=-1, keepdims=True)
    return centered * lax.rsqrt(row_var + 1e-05) * gain + bias


def local(
    hidden_in, norm_gain, norm_bias, w_query, w_keyval, bias_query, bias_keyval,
    cache_keys, cache_values, cache_lengths, owner_slot, w_out, bias_out,
):
    row_id = lax.axis_index("row")
    col_id = lax.axis_index("col")
    group_len = hidden_in.shape[0]
    req_count = owner_slot.shape[0]
    slot_ids = jnp.arange(req_count, dtype=jnp.int32)
    is_owner = owner_slot[:, None] == slot_ids[None, :]
    inverse = jnp.sum(jnp.where(is_owner, slot_ids[:, None], 0), axis=0)
    length = cache_lengths[inverse[row_id]].reshape(1)
    share = lax.dynamic_slice_in_dim(hidden_in, col_id * 32, 32, 0).astype(F32)
    normed = normalize(share, norm_gain, norm_bias).astype(BF16)
    act = normed.reshape(32, 4, 4, 448).transpose(2, 0, 1, 3).reshape(4, 32, 1792)
    bias = jnp.concatenate([bias_query[None], bias_keyval], axis=0)
    query, new_k, new_v = project(inverse, act, w_query, w_keyval.transpose(1, 0, 2), bias)
    attended = attend(length, query, cache_keys, cache_values, new_k, new_v)
    halves = combine(owner_slot, attended, w_out)
    summed = jnp.concatenate([halves[0], halves[1]], axis=1).astype(F32)
    out_cols = summed.shape[1]
    residual = lax.dynamic_slice_in_dim(hidden_in, col_id * out_cols, out_cols, 1).astype(F32)
    hidden_out = (summed + bias_out + residual).astype(BF16)
    return (hidden_out, new_k[None], new_v[None])


def solution(mesh):
    placed = (
        P("row", None), P(), P(), P("row", "col"), P("row", None, "col"), P("col"), P(None, "col"),
        P("row", None, "col"), P("row", None, "col"), P(), P(), P("col", "row"), P("col"),
    )
    return jax.shard_map(
        local,
        mesh=mesh,
        in_specs=placed,
        out_specs=(P("row", "col"), P("row", None, "col"), P("row", None, "col")),
        check_vma=False,
    )
```

```python
import jax
import jax.numpy as jnp
from jax import lax
from jax.experimental import pallas as pl
from jax.experimental.pallas import tpu as pltpu
from jax.sharding import PartitionSpec as P

HEAD = 128
MESH = pl.DeviceIdType.MESH
BF16 = jnp.bfloat16
F32 = jnp.float32
NEG = -1e30


def place():
    row, col = lax.axis_index("row"), lax.axis_index("col")
    return row, col, lax.div(row, 4), lax.rem(row, 4), lax.div(col, 2), lax.rem(col, 2)


def send(src, dst, send_sem, recv_sem, row, col):
    copy = pltpu.make_async_remote_copy(
        src_ref=src,
        dst_ref=dst,
        send_sem=send_sem,
        recv_sem=recv_sem,
        device_id=(row, col),
        device_id_type=MESH,
    )
    copy.start()
    return copy


def greet(peers):
    barrier = pltpu.get_barrier_semaphore()
    for row, col in peers:
        pl.semaphore_signal(barrier, inc=1, device_id=(row, col), device_id_type=MESH)
    pl.semaphore_wait(barrier, len(peers))


class Ring:
    def __init__(self, me, device, block, half, send_sem, recv_sem):
        self.me, self.device, self.block, self.half = me, device, block, half
        self.send_sem, self.recv_sem = send_sem, recv_sem
        self.copies = []

    def start(self):
        for i, step in enumerate((1, 3)):
            to = self.device(lax.rem(self.me + step, 4))
            view = self.block(self.me)
            self.copies.append(send(view, view, self.send_sem(i), self.recv_sem(i), *to))

    def forward(self):
        for i, step in enumerate((1, 3)):
            self.copies[i].wait_recv()
            to = self.device(lax.rem(self.me + step, 4))
            view = self.half(lax.rem(self.me + 4 - step, 4), i)
            self.copies.append(send(view, view, self.send_sem(2 + i), self.recv_sem(2 + i), *to))

    def finish(self):
        for copy in self.copies[2:]:
            copy.wait_recv()

    def drain(self):
        for copy in self.copies:
            copy.wait_send()


PARTS = 9
WIDE = 256
KEYS = 1024
BLOCKS = 4096 // KEYS


def front_kernel(
    owner_ref, len_ref, hid_ref, gain_ref, shift_ref, wq_ref, wkv_ref, bq_ref, bkv_ref, ck_ref, cv_ref,
    k_ref, v_ref, att_ref,
    hbuf, act, ybuf, abuf, wbuf, psend, rbuf, acc, qbuf, kbuf, vbuf, m_s, l_s, o_s,
    hsem, lsem, ksem, vsem, xs, xr, ys, yr, zs, zr, cs, cr, ws, wr, ps, pr,
):
    row, col, y, x, z, core = place()
    at = lambda yy, xx: yy * 4 + xx
    other = z * 2 + (1 - core)
    peers = [(at(y, lax.rem(x + d, 4)), col) for d in (1, 2, 3)]
    peers += [(at(lax.rem(y + d, 4), x), col) for d in (1, 3)]
    peers += [(row, lax.rem(z + d, 4) * 2 + core) for d in (1, 3)]
    peers += [(row, other)]

    def request_of(slot):
        request = 0
        for i in range(16):
            request = jnp.where(owner_ref[i] == slot, i, request)
        return request

    hcopy = pltpu.make_async_copy(hid_ref.at[pl.ds(col * 32, 32)], hbuf, hsem)
    hcopy.start()
    local = []
    for p in range(PARTS):
        lanes = pl.ds(p % 3 * WIDE, WIDE)
        source = wq_ref.at[:, lanes] if p < 3 else wkv_ref.at[p // 3 - 1, :, lanes]
        local.append(pltpu.make_async_copy(source, wbuf.at[p, y], lsem.at[p]))
        local[p].start()

    def fetch(n):
        pair, block, slot = lax.div(n, BLOCKS), lax.rem(n, BLOCKS), lax.rem(n, 2)
        place_of = (pl.ds(block * KEYS, KEYS), pl.ds(pl.multiple_of(pair * WIDE, WIDE), WIDE))
        return (
            pltpu.make_async_copy(ck_ref.at[place_of], kbuf.at[slot], ksem.at[slot]),
            pltpu.make_async_copy(cv_ref.at[place_of], vbuf.at[slot], vsem.at[slot]),
        )

    for copy in fetch(jnp.int32(0)):
        copy.start()
    greet(peers)

    wring = [
        Ring(
            y,
            lambda o: (at(o, x), col),
            lambda o, p=p: wbuf.at[p, o],
            lambda o, i, p=p: wbuf.at[p, o, pl.ds(224 * i, 224)],
            lambda i, p=p: ws.at[p, i],
            lambda i, p=p: wr.at[p, i],
        )
        for p in range(PARTS)
    ]

    def launch(p):
        if p < PARTS:
            local[p].wait()
            wring[p].start()

    def pump(p):
        wring[p].forward()
        launch(p + 2)

    launch(0)
    hcopy.wait()
    inputs = hbuf[...].astype(F32)
    width = inputs.shape[1]
    centered = inputs - jnp.sum(inputs, axis=1, keepdims=True) * (1.0 / width)
    var = jnp.sum(centered * centered, axis=1, keepdims=True) * (1.0 / width)
    normed = (centered * lax.rsqrt(var + 1e-05) * gain_ref[...] + shift_ref[...]).astype(BF16)
    for xx in range(4):
        for yy in range(4):
            begin = (yy * 4 + xx) * 448
            act[xx, :, yy * 448 : (yy + 1) * 448] = normed[:, begin : begin + 448]
    xcopies = []
    for d in (1, 2, 3):
        to = lax.rem(x + d, 4)
        xcopies.append(
            send(act.at[to], ybuf.at[y, x], xs.at[d - 1], xr.at[d - 1], at(y, to), col)
        )
    ybuf[y, x] = act[x]
    for copy in xcopies:
        copy.wait_recv()
    yring = Ring(
        y,
        lambda o: (at(o, x), col),
        lambda o: ybuf.at[o],
        lambda o, i: ybuf.at[o, pl.ds(2 * i, 2)],
        lambda i: ys.at[i],
        lambda i: yr.at[i],
    )
    yring.start()
    launch(1)
    yring.forward()
    pump(0)
    yring.finish()
    for s in range(4):
        request = request_of(y * 4 + s)
        abuf[s, col] = ybuf[lax.div(request, 4), lax.rem(request, 4)]
    zring = Ring(
        z,
        lambda o: (row, o * 2 + core),
        lambda o: abuf.at[:, o * 2 + core],
        lambda o, i: abuf.at[pl.ds(2 * i, 2), o * 2 + core],
        lambda i: zs.at[i],
        lambda i: zr.at[i],
    )
    zring.start()
    ccopies = []

    def across(view):
        i = len(ccopies)
        ccopies.append(send(view, view, cs.at[i], cr.at[i], row, other))

    across(zring.block(z))
    pump(1)
    zring.forward()
    across(zring.block(lax.rem(z + 3, 4)))
    across(zring.block(lax.rem(z + 1, 4)))
    pump(2)
    zring.finish()
    across(zring.block(lax.rem(z + 2, 4)))
    for copy in ccopies:
        copy.wait_recv()

    def multiply(part):
        wring[part].finish()

        def block(i, carry):
            to = lax.rem(x + i + 1, 4)
            out = jnp.dot(
                abuf[to].reshape(256, 1792),
                wbuf[part].reshape(1792, WIDE),
                preferred_element_type=F32,
            )
            acc[part] = out
            psend[part, i] = out.astype(BF16)

            @pl.when(i < 3)
            def _():
                send(
                    psend.at[part, i], rbuf.at[part, i], ps.at[part, i], pr.at[part, i],
                    at(y, to), col,
                )

            return carry

        lax.fori_loop(0, 4, block, 0)

    def arrived(part, i):
        return pltpu.make_async_remote_copy(
            src_ref=psend.at[part, i],
            dst_ref=rbuf.at[part, i],
            send_sem=ps.at[part, i],
            recv_sem=pr.at[part, i],
            device_id=(at(y, lax.rem(x + i + 1, 4)), col),
            device_id_type=MESH,
        )

    def total(part):
        for i in range(3):
            arrived(part, i).wait_recv()
        out = acc[part]
        for i in range(3):
            out = out + rbuf[part, i].astype(F32)
        lanes = slice(part % 3 * WIDE, (part % 3 + 1) * WIDE)
        if part < 3:
            qbuf[part] = ((out + bq_ref[:, lanes]) * (HEAD**-0.5)).astype(BF16)
        elif part < 6:
            k_ref[:, lanes] = (out + bkv_ref[0:1, lanes]).astype(BF16)
        else:
            v_ref[:, lanes] = (out + bkv_ref[1:2, lanes]).astype(BF16)

    m_s[...] = jnp.full_like(m_s, NEG)
    l_s[...] = jnp.zeros_like(l_s)
    o_s[...] = jnp.zeros_like(o_s)
    length = len_ref[request_of(row)]

    def visit(pair, keys, values, bias):
        for j in range(2):
            h = pair * 2 + j
            lanes = slice(j * HEAD, (j + 1) * HEAD)
            scores = lax.dot_general(
                qbuf[pair, :, lanes], keys[:, lanes], (((1,), (1,)), ((), ())),
                preferred_element_type=F32,
            )
            scores = scores + bias
            old = m_s[h]
            new = jnp.maximum(old, jnp.max(scores, axis=1, keepdims=True))
            probs = jnp.exp(scores - new)
            factor = jnp.exp(old - new)
            m_s[h] = new
            l_s[h] = l_s[h] * factor + jnp.sum(probs, axis=1, keepdims=True)
            o_s[h] = o_s[h] * factor + jnp.dot(
                probs.astype(BF16), values[:, lanes], preferred_element_type=F32
            )

    def cached(pair, begin, end):
        def step(block, carry):
            n = pair * BLOCKS + block
            slot = lax.rem(n, 2)
            for copy in fetch(n):
                copy.wait()

            @pl.when(n + 1 < 3 * BLOCKS)
            def _():
                for copy in fetch(n + 1):
                    copy.start()

            pos = block * KEYS + lax.broadcasted_iota(jnp.int32, (1, KEYS), 1)
            visit(pair, kbuf[slot], vbuf[slot], jnp.where(pos < length, 0.0, NEG))
            return carry

        lax.fori_loop(begin, end, step, 0)

    late = lax.broadcasted_iota(jnp.int32, (256, 256), 1) > lax.broadcasted_iota(
        jnp.int32, (256, 256), 0
    )
    causal = jnp.where(late, NEG, 0.0)

    def fresh(pair):
        lanes = slice(pair * WIDE, (pair + 1) * WIDE)
        visit(pair, k_ref[:, lanes], v_ref[:, lanes], causal)
        for h in (pair * 2, pair * 2 + 1):
            att_ref[:, h * HEAD : (h + 1) * HEAD] = (o_s[h] / l_s[h]).astype(BF16)

    pump(3)
    multiply(0)
    multiply(1)
    pump(4)
    multiply(2)
    total(0)
    cached(0, 0, BLOCKS // 2)
    pump(5)
    multiply(3)
    total(1)
    cached(0, BLOCKS // 2, BLOCKS)
    pump(6)
    multiply(4)
    total(2)
    cached(1, 0, BLOCKS // 2)
    pump(7)
    multiply(5)
    cached(1, BLOCKS // 2, BLOCKS)
    pump(8)
    multiply(6)
    total(3)
    total(4)
    cached(2, 0, BLOCKS // 2)
    multiply(7)
    total(5)
    multiply(8)
    total(6)
    cached(2, BLOCKS // 2, BLOCKS)
    fresh(0)
    total(7)
    fresh(1)
    total(8)
    fresh(2)

    for copy in xcopies + ccopies:
        copy.wait_send()
    for ring in [yring, zring] + wring:
        ring.drain()
    for part in range(PARTS):
        for i in range(3):
            arrived(part, i).wait_send()


def front(owner_slot, lengths, hidden, gain, shift, wq, wkv, bq, bkv, cache_k, cache_v):
    dma = pltpu.SemaphoreType.DMA
    vmem = pl.BlockSpec(memory_space=pltpu.VMEM)
    smem = pl.BlockSpec(memory_space=pltpu.SMEM)
    hbm = pl.BlockSpec(memory_space=pl.ANY)
    out = jax.ShapeDtypeStruct((256, 768), BF16)
    return pl.pallas_call(
        front_kernel,
        out_shape=(out, out, out),
        in_specs=[smem, smem, hbm, vmem, vmem, hbm, hbm, vmem, vmem, hbm, hbm],
        out_specs=(vmem, vmem, vmem),
        scratch_shapes=[
            pltpu.VMEM((32, 7168), BF16),
            pltpu.VMEM((4, 32, 1792), BF16),
            pltpu.VMEM((4, 4, 32, 1792), BF16),
            pltpu.VMEM((4, 8, 32, 1792), BF16),
            pltpu.VMEM((PARTS, 4, 448, WIDE), BF16),
            pltpu.VMEM((PARTS, 4, 256, WIDE), BF16),
            pltpu.VMEM((PARTS, 3, 256, WIDE), BF16),
            pltpu.VMEM((PARTS, 256, WIDE), F32),
            pltpu.VMEM((3, 256, WIDE), BF16),
            pltpu.VMEM((2, KEYS, WIDE), BF16),
            pltpu.VMEM((2, KEYS, WIDE), BF16),
            pltpu.VMEM((6, 256, 1), F32),
            pltpu.VMEM((6, 256, 1), F32),
            pltpu.VMEM((6, 256, HEAD), F32),
            dma,
            dma((PARTS,)),
            dma((2,)), dma((2,)),
            dma((3,)), dma((3,)),
            dma((4,)), dma((4,)),
            dma((4,)), dma((4,)),
            dma((4,)), dma((4,)),
            dma((PARTS, 4)), dma((PARTS, 4)),
            dma((PARTS, 3)), dma((PARTS, 3)),
        ],
        compiler_params=pltpu.CompilerParams(
            collective_id=0, has_side_effects=True, vmem_limit_bytes=58 * 2**20
        ),
        name="front",
    )(owner_slot, lengths, hidden, gain, shift, wq, wkv, bq, bkv, cache_k, cache_v)


def out_kernel(
    own_ref, att_ref, w_ref, out_ref,
    ag0, ag1, csend, crecv, mine, zsend, zrecv, fsend, frecv,
    lsem, as_, ar, bs, br, cs, cr, zs, zr, fs, fr,
):
    row, col, y, x, z, core = place()
    at = lambda yy, xx: yy * 4 + xx
    other = z * 2 + (1 - core)
    peers = [(at(y, lax.rem(x + d, 4)), col) for d in (1, 3)]
    peers += [(at(lax.rem(y + d, 4), x), col) for d in (1, 3)]
    peers += [(row, lax.rem(z + d, 4) * 2 + core) for d in (1, 2, 3)]
    peers += [(row, other)]
    targets = [(2 * col + i, lax.div(row, 2)) for i in (0, 1)]
    barrier = pltpu.get_barrier_semaphore()
    selves = [jnp.logical_and(t[0] == row, t[1] == col) for t in targets]

    ag = (ag0, ag1)
    local = []
    for t in range(2):
        for h in range(2):
            local.append(
                pltpu.make_async_copy(
                    att_ref.at[pl.ds(t * 128 + h * 64, 64)], ag[t].at[h, y, x], lsem.at[t, h]
                )
            )
            local[-1].start()
    for r, c in peers:
        pl.semaphore_signal(barrier, inc=1, device_id=(r, c), device_id_type=MESH)
    for i in range(2):

        @pl.when(jnp.logical_not(selves[i]))
        def _():
            pl.semaphore_signal(barrier, inc=1, device_id=targets[i], device_id_type=MESH)

    alone = (lax.div(row, 2) == col).astype(jnp.int32)
    pl.semaphore_wait(barrier, len(peers) + 2 - alone)

    for copy in local:
        copy.wait()

    def xline(o):
        return (at(y, o), col)

    def yline(o):
        return (at(o, x), col)

    first, second = [], []
    for t in range(2):
        sem = lambda s, p, t=t: (lambda i: s.at[t, p, i])
        first.append((
            Ring(x, xline, lambda o, t=t: ag[t].at[0, y, o],
                 lambda o, i, t=t: ag[t].at[0, y, o, pl.ds(32 * i, 32)], sem(as_, 0), sem(ar, 0)),
            Ring(y, yline, lambda o, t=t: ag[t].at[1, o, x],
                 lambda o, i, t=t: ag[t].at[1, o, x, pl.ds(32 * i, 32)], sem(bs, 0), sem(br, 0)),
        ))
        second.append((
            Ring(y, yline, lambda o, t=t: ag[t].at[0, o],
                 lambda o, i, t=t: ag[t].at[0, o, pl.ds(2 * i, 2)], sem(as_, 1), sem(ar, 1)),
            Ring(x, xline, lambda o, t=t: ag[t].at[1, :, o],
                 lambda o, i, t=t: ag[t].at[1, pl.ds(2 * i, 2), o], sem(bs, 1), sem(br, 1)),
        ))

    def each(rings, what):
        for ring in rings:
            getattr(ring, what)()

    each(first[0], "start")
    each(first[0], "forward")
    each(first[1], "start")
    each(first[0], "finish")
    each(second[0], "start")
    each(first[1], "forward")
    each(first[1], "finish")
    each(second[0], "forward")
    each(second[1], "start")

    def partial(t, g, to_core):
        rows = []
        for j in range(4):
            owner = own_ref[g * 8 + j // 2 * 4 + to_core * 2 + j % 2]
            oy, ox = lax.div(owner, 4), lax.rem(owner, 4)
            rows += [ag[t][0, oy, ox], ag[t][1, oy, ox]]
        out = jnp.dot(jnp.concatenate(rows, axis=0), w_ref[...], preferred_element_type=F32)
        return out.reshape(4, 128, 448)

    copies = []

    def reduce(t):
        def away(g, carry):
            csend[t, pl.ds(g * 4, 4)] = partial(t, g, 1 - core).astype(BF16)
            return carry

        lax.fori_loop(0, 2, away, 0)
        ccopy = send(csend.at[t], crecv.at[t], cs.at[t], cr.at[t], row, other)

        def stay(g, carry):
            mine[t, pl.ds(g * 4, 4)] = partial(t, g, core)
            return carry

        lax.fori_loop(0, 2, stay, 0)
        ccopy.wait_recv()
        copies.append(ccopy)
        zcopies = []
        for d in (1, 2, 3):
            to = lax.rem(z + d, 4)
            for i in range(2):
                zsend[t, d - 1, i] = (
                    mine[t, to * 2 + i] + crecv[t, to * 2 + i].astype(F32)
                ).astype(BF16)
            zcopies.append(
                send(zsend.at[t, d - 1], zrecv.at[t, d - 1], zs.at[t, d - 1], zr.at[t, d - 1],
                     row, to * 2 + core)
            )
        copies.extend(zcopies)
        return zcopies

    def hand_over(t, zcopies):
        for copy in zcopies:
            copy.wait_recv()
        for i in range(2):
            total = mine[t, z * 2 + i] + crecv[t, z * 2 + i].astype(F32)
            for d in range(3):
                total = total + zrecv[t, d, i].astype(F32)
            fsend[t, i] = total.astype(BF16)

            @pl.when(jnp.logical_not(selves[i]))
            def _():
                last(t, i).start()

            @pl.when(selves[i])
            def _():
                frecv[t, lax.rem(row, 2)] = fsend[t, i]

    def last(t, i):
        return pltpu.make_async_remote_copy(
            src_ref=fsend.at[t, i],
            dst_ref=frecv.at[t, lax.rem(row, 2)],
            send_sem=fs.at[t, i],
            recv_sem=fr.at[t, lax.rem(row, 2)],
            device_id=targets[i],
            device_id_type=MESH,
        )

    each(second[0], "finish")
    z0 = reduce(0)
    each(second[1], "forward")
    hand_over(0, z0)
    each(second[1], "finish")
    z1 = reduce(1)
    hand_over(1, z1)

    for t in range(2):
        for k in range(2):

            @pl.when(jnp.logical_not(selves[k]))
            def _():
                pltpu.make_async_remote_copy(
                    src_ref=fsend.at[t, k], dst_ref=frecv.at[t, k], send_sem=fs.at[t, k],
                    recv_sem=fr.at[t, k], device_id=targets[k], device_id_type=MESH,
                ).wait_recv()

            out_ref[k, pl.ds(t * 128, 128)] = frecv[t, k]
    for t in range(2):
        for i in range(2):

            @pl.when(jnp.logical_not(selves[i]))
            def _():
                last(t, i).wait_send()

    for copy in copies:
        copy.wait_send()
    for pair in first + second:
        each(pair, "drain")


def combine(owner_slot, attended, w_out):
    dma = pltpu.SemaphoreType.DMA
    vmem = pl.BlockSpec(memory_space=pltpu.VMEM)
    return pl.pallas_call(
        out_kernel,
        out_shape=jax.ShapeDtypeStruct((2, 256, 448), BF16),
        in_specs=[pl.BlockSpec(memory_space=pltpu.SMEM), vmem, vmem],
        out_specs=vmem,
        scratch_shapes=[
            pltpu.VMEM((2, 4, 4, 64, 768), BF16),
            pltpu.VMEM((2, 4, 4, 64, 768), BF16),
            pltpu.VMEM((2, 8, 128, 448), BF16),
            pltpu.VMEM((2, 8, 128, 448), BF16),
            pltpu.VMEM((2, 8, 128, 448), F32),
            pltpu.VMEM((2, 3, 2, 128, 448), BF16),
            pltpu.VMEM((2, 3, 2, 128, 448), BF16),
            pltpu.VMEM((2, 2, 128, 448), BF16),
            pltpu.VMEM((2, 2, 128, 448), BF16),
            dma((2, 2)),
            dma((2, 2, 4)), dma((2, 2, 4)),
            dma((2, 2, 4)), dma((2, 2, 4)),
            dma((2,)), dma((2,)),
            dma((2, 3)), dma((2, 3)),
            dma((2, 2)), dma((2, 2)),
        ],
        compiler_params=pltpu.CompilerParams(
            collective_id=1, has_side_effects=True, vmem_limit_bytes=56 * 2**20
        ),
        name="out",
    )(owner_slot, attended, w_out)


def local(
    hidden_in, norm_gain, norm_bias, w_query, w_keyval, bias_query, bias_keyval,
    cache_keys, cache_values, cache_lengths, owner_slot, w_out, bias_out,
):
    col_id = lax.axis_index("col")
    new_k, new_v, attended = front(
        owner_slot, cache_lengths, hidden_in, norm_gain[None], norm_bias[None],
        w_query, w_keyval.transpose(1, 0, 2), bias_query[None], bias_keyval,
        cache_keys[0], cache_values[0],
    )
    halves = combine(owner_slot, attended, w_out)
    summed = jnp.concatenate([halves[0], halves[1]], axis=1).astype(F32)
    out_cols = summed.shape[1]
    residual = lax.dynamic_slice_in_dim(hidden_in, col_id * out_cols, out_cols, 1).astype(F32)
    hidden_out = (summed + bias_out + residual).astype(BF16)
    return (hidden_out, new_k[None], new_v[None])


def solution(mesh):
    placed = (
        P("row", None), P(), P(), P("row", "col"), P("row", None, "col"), P("col"), P(None, "col"),
        P("row", None, "col"), P("row", None, "col"), P(), P(), P("col", "row"), P("col"),
    )
    return jax.shard_map(
        local,
        mesh=mesh,
        in_specs=placed,
        out_specs=(P("row", "col"), P("row", None, "col"), P("row", None, "col")),
        check_vma=False,
    )
```

```python
import jax
import jax.numpy as jnp
from jax import lax
from jax.experimental import pallas as pl
from jax.experimental.pallas import tpu as pltpu
from jax.sharding import PartitionSpec as P

HEAD = 128
MESH = pl.DeviceIdType.MESH
BF16 = jnp.bfloat16
F32 = jnp.float32
NEG = -1e30


def place():
    row, col = lax.axis_index("row"), lax.axis_index("col")
    return row, col, lax.div(row, 4), lax.rem(row, 4), lax.div(col, 2), lax.rem(col, 2)


def send(src, dst, send_sem, recv_sem, row, col):
    copy = pltpu.make_async_remote_copy(
        src_ref=src,
        dst_ref=dst,
        send_sem=send_sem,
        recv_sem=recv_sem,
        device_id=(row, col),
        device_id_type=MESH,
    )
    copy.start()
    return copy


def greet(peers):
    barrier = pltpu.get_barrier_semaphore()
    for row, col in peers:
        pl.semaphore_signal(barrier, inc=1, device_id=(row, col), device_id_type=MESH)
    pl.semaphore_wait(barrier, len(peers))


class Ring:
    def __init__(self, me, device, block, half, send_sem, recv_sem):
        self.me, self.device, self.block, self.half = me, device, block, half
        self.send_sem, self.recv_sem = send_sem, recv_sem
        self.copies = []

    def start(self):
        for i, step in enumerate((1, 3)):
            to = self.device(lax.rem(self.me + step, 4))
            view = self.block(self.me)
            self.copies.append(send(view, view, self.send_sem(i), self.recv_sem(i), *to))

    def forward(self):
        for i, step in enumerate((1, 3)):
            self.copies[i].wait_recv()
            to = self.device(lax.rem(self.me + step, 4))
            view = self.half(lax.rem(self.me + 4 - step, 4), i)
            self.copies.append(send(view, view, self.send_sem(2 + i), self.recv_sem(2 + i), *to))

    def finish(self):
        for copy in self.copies[2:]:
            copy.wait_recv()

    def drain(self):
        for copy in self.copies:
            copy.wait_send()


ORDER = ((0, 0), (0, 1), (0, 2), (1, 0), (2, 0), (1, 1), (2, 1), (1, 2), (2, 2))
PARTS = len(ORDER)
WIDE = 256
KEYS = 1024
BLOCKS = 4096 // KEYS


def layer_kernel(
    owner_ref, len_ref, hid_ref, gain_ref, shift_ref, wq_ref, wkv_ref, bq_ref, bkv_ref, ck_ref, cv_ref,
    wout_ref, bo_ref,
    out_ref, k_ref, v_ref,
    hbuf, act, ybuf, abuf, wbuf, psend, rbuf, acc, qbuf, kbuf, vbuf, m_s, l_s, o_s,
    asend, ag0, ag1, ag2, wo, lhs, oacc, fsend, frecv, res,
    hsem, lsem, ksem, vsem, xs, xr, ys, yr, zs, zr, cs, cr, ws, wr, ps, pr,
    osem, rsem, os_, or_, ocs, ocr, hs, hr, gs, gr, fs, fr,
):
    row, col, y, x, z, core = place()
    at = lambda yy, xx: yy * 4 + xx
    other = z * 2 + (1 - core)
    peers = [(at(y, lax.rem(x + d, 4)), col) for d in (1, 2, 3)]
    peers += [(at(lax.rem(y + d, 4), x), col) for d in (1, 3)]
    peers += [(row, lax.rem(z + d, 4) * 2 + core) for d in (1, 3)]
    peers += [(row, other)]

    def request_of(slot):
        request = 0
        for i in range(16):
            request = jnp.where(owner_ref[i] == slot, i, request)
        return request

    hcopy = pltpu.make_async_copy(hid_ref.at[pl.ds(col * 32, 32)], hbuf, hsem)
    hcopy.start()
    local = []
    for p in range(PARTS):
        kind, pair = ORDER[p]
        lanes = pl.ds(pair * WIDE, WIDE)
        source = wq_ref.at[:, lanes] if kind == 0 else wkv_ref.at[kind - 1, :, lanes]
        local.append(pltpu.make_async_copy(source, wbuf.at[p, y], lsem.at[p]))
        local[p].start()

    def fetch(n):
        pair, block, slot = lax.div(n, BLOCKS), lax.rem(n, BLOCKS), lax.rem(n, 2)
        place_of = (pl.ds(block * KEYS, KEYS), pl.ds(pl.multiple_of(pair * WIDE, WIDE), WIDE))
        return (
            pltpu.make_async_copy(ck_ref.at[place_of], kbuf.at[slot], ksem.at[slot]),
            pltpu.make_async_copy(cv_ref.at[place_of], vbuf.at[slot], vsem.at[slot]),
        )

    for copy in fetch(jnp.int32(0)):
        copy.start()
    ocopy = pltpu.make_async_copy(wout_ref, wo.at[col], osem)
    ocopy.start()
    rcopy = pltpu.make_async_copy(hid_ref.at[:, pl.ds(pl.multiple_of(col * 896, 128), 896)], res, rsem)
    rcopy.start()
    greet(peers)

    wring = [
        Ring(
            y,
            lambda o: (at(o, x), col),
            lambda o, p=p: wbuf.at[p, o],
            lambda o, i, p=p: wbuf.at[p, o, pl.ds(224 * i, 224)],
            lambda i, p=p: ws.at[p, i],
            lambda i, p=p: wr.at[p, i],
        )
        for p in range(PARTS)
    ]

    def launch(p):
        if p < PARTS:
            local[p].wait()
            wring[p].start()

    def pump(p):
        wring[p].forward()
        launch(p + 2)

    launch(0)
    hcopy.wait()
    inputs = hbuf[...].astype(F32)
    width = inputs.shape[1]
    centered = inputs - jnp.sum(inputs, axis=1, keepdims=True) * (1.0 / width)
    var = jnp.sum(centered * centered, axis=1, keepdims=True) * (1.0 / width)
    normed = (centered * lax.rsqrt(var + 1e-05) * gain_ref[...] + shift_ref[...]).astype(BF16)
    for xx in range(4):
        for yy in range(4):
            begin = (yy * 4 + xx) * 448
            act[xx, :, yy * 448 : (yy + 1) * 448] = normed[:, begin : begin + 448]
    xcopies = []
    for d in (1, 2, 3):
        to = lax.rem(x + d, 4)
        xcopies.append(
            send(act.at[to], ybuf.at[y, x], xs.at[d - 1], xr.at[d - 1], at(y, to), col)
        )
    ybuf[y, x] = act[x]
    for copy in xcopies:
        copy.wait_recv()
    yring = Ring(
        y,
        lambda o: (at(o, x), col),
        lambda o: ybuf.at[o],
        lambda o, i: ybuf.at[o, pl.ds(2 * i, 2)],
        lambda i: ys.at[i],
        lambda i: yr.at[i],
    )
    yring.start()
    launch(1)
    yring.forward()
    pump(0)
    yring.finish()
    for s in range(4):
        request = request_of(y * 4 + s)
        abuf[s, col] = ybuf[lax.div(request, 4), lax.rem(request, 4)]
    zring = Ring(
        z,
        lambda o: (row, o * 2 + core),
        lambda o: abuf.at[:, o * 2 + core],
        lambda o, i: abuf.at[pl.ds(2 * i, 2), o * 2 + core],
        lambda i: zs.at[i],
        lambda i: zr.at[i],
    )
    zring.start()
    ccopies = []

    def across(view):
        i = len(ccopies)
        ccopies.append(send(view, view, cs.at[i], cr.at[i], row, other))

    across(zring.block(z))
    pump(1)
    zring.forward()
    across(zring.block(lax.rem(z + 3, 4)))
    across(zring.block(lax.rem(z + 1, 4)))
    pump(2)
    zring.finish()
    across(zring.block(lax.rem(z + 2, 4)))
    oring = Ring(
        z,
        lambda o: (row, o * 2 + core),
        lambda o: wo.at[o * 2 + core],
        lambda o, i: wo.at[o * 2 + core, pl.ds(384 * i, 384)],
        lambda i: os_.at[i],
        lambda i: or_.at[i],
    )
    ocopy.wait()
    oring.start()
    ocopies = []

    def across_out(o):
        i, view = len(ocopies), oring.block(o)
        ocopies.append(send(view, view, ocs.at[i], ocr.at[i], row, other))

    for copy in ccopies:
        copy.wait_recv()

    def multiply(part):
        wring[part].finish()

        def block(i, carry):
            to = lax.rem(x + i + 1, 4)
            out = jnp.dot(
                abuf[to].reshape(256, 1792),
                wbuf[part].reshape(1792, WIDE),
                preferred_element_type=F32,
            )
            acc[part] = out

            @pl.when(i < 3)
            def _():
                psend[part, i] = out.astype(BF16)
                send(
                    psend.at[part, i], rbuf.at[part, i], ps.at[part, i], pr.at[part, i],
                    at(y, to), col,
                )

            return carry

        lax.fori_loop(0, 4, block, 0)

    def arrived(part, i):
        return pltpu.make_async_remote_copy(
            src_ref=psend.at[part, i],
            dst_ref=rbuf.at[part, i],
            send_sem=ps.at[part, i],
            recv_sem=pr.at[part, i],
            device_id=(at(y, lax.rem(x + i + 1, 4)), col),
            device_id_type=MESH,
        )

    def total(part):
        for i in range(3):
            arrived(part, i).wait_recv()
        out = acc[part]
        for i in range(3):
            out = out + rbuf[part, i].astype(F32)
        kind, pair = ORDER[part]
        lanes = slice(pair * WIDE, (pair + 1) * WIDE)
        if kind == 0:
            qbuf[pair] = ((out + bq_ref[:, lanes]) * (HEAD**-0.5)).astype(BF16)
        else:
            to_ref = (k_ref, v_ref)[kind - 1]
            to_ref[:, lanes] = (out + bkv_ref[kind - 1 : kind, lanes]).astype(BF16)

    m_s[...] = jnp.full_like(m_s, NEG)
    l_s[...] = jnp.zeros_like(l_s)
    o_s[...] = jnp.zeros_like(o_s)
    length = len_ref[request_of(row)]

    def visit(pair, keys, values, bias):
        for j in range(2):
            h = pair * 2 + j
            lanes = slice(j * HEAD, (j + 1) * HEAD)
            scores = lax.dot_general(
                qbuf[pair, :, lanes], keys[:, lanes], (((1,), (1,)), ((), ())),
                preferred_element_type=F32,
            )
            scores = scores + bias
            old = m_s[h]
            new = jnp.maximum(old, jnp.max(scores, axis=1, keepdims=True))
            probs = jnp.exp(scores - new)
            factor = jnp.exp(old - new)
            m_s[h] = new
            l_s[h] = l_s[h] * factor + jnp.sum(probs, axis=1, keepdims=True)
            o_s[h] = o_s[h] * factor + jnp.dot(
                probs.astype(BF16), values[:, lanes], preferred_element_type=F32
            )

    def cached(pair, begin, end):
        def step(block, carry):
            n = pair * BLOCKS + block
            slot = lax.rem(n, 2)
            for copy in fetch(n):
                copy.wait()

            @pl.when(n + 1 < 3 * BLOCKS)
            def _():
                for copy in fetch(n + 1):
                    copy.start()

            pos = block * KEYS + lax.broadcasted_iota(jnp.int32, (1, KEYS), 1)
            visit(pair, kbuf[slot], vbuf[slot], jnp.where(pos < length, 0.0, NEG))
            return carry

        lax.fori_loop(begin, end, step, 0)

    late = lax.broadcasted_iota(jnp.int32, (256, 256), 1) > lax.broadcasted_iota(
        jnp.int32, (256, 256), 0
    )
    causal = jnp.where(late, NEG, 0.0)

    def fresh(pair):
        lanes = slice(pair * WIDE, (pair + 1) * WIDE)
        visit(pair, k_ref[:, lanes], v_ref[:, lanes], causal)
        for j in range(2):
            h = pair * 2 + j
            done = (o_s[h] / l_s[h]).astype(BF16)
            asend[pair, :, :, :, j * HEAD : (j + 1) * HEAD] = done.reshape(8, 2, 16, HEAD)

    ag = (ag0, ag1, ag2)
    hcopies = [[], [], []]

    def share(pair):
        mine = ag[pair]
        for d in range(1, 8):
            to = lax.rem(col + d, 8)
            hcopies[pair].append(
                send(asend.at[pair, to], mine.at[:, y, x, col], hs.at[pair, d - 1], hr.at[pair, d - 1],
                     row, to)
            )
        mine[:, y, x, col] = asend[pair, col]

    xline = lambda o: (at(y, o), col)
    yline = lambda o: (at(o, x), col)

    def rings(pair):
        mine = ag[pair]

        def sems(phase, k):
            return (lambda i: gs.at[pair, phase, k, i]), (lambda i: gr.at[pair, phase, k, i])

        if pair < 2:
            return (
                [Ring(y, yline, lambda o: mine.at[:, o, x], lambda o, i: mine.at[i, o, x], *sems(0, 0))],
                [Ring(x, xline, lambda o: mine.at[:, :, o], lambda o, i: mine.at[i, :, o], *sems(1, 0))],
            )
        return (
            [
                Ring(x, xline, lambda o: mine.at[0, y, o],
                     lambda o, i: mine.at[0, y, o, pl.ds(4 * i, 4)], *sems(0, 0)),
                Ring(y, yline, lambda o: mine.at[1, o, x],
                     lambda o, i: mine.at[1, o, x, pl.ds(4 * i, 4)], *sems(0, 1)),
            ],
            [
                Ring(y, yline, lambda o: mine.at[0, o],
                     lambda o, i: mine.at[0, o, pl.ds(2 * i, 2)], *sems(1, 0)),
                Ring(x, xline, lambda o: mine.at[1, :, o],
                     lambda o, i: mine.at[1, pl.ds(2 * i, 2), o], *sems(1, 1)),
            ],
        )

    gather = [rings(pair) for pair in range(3)]

    def stage(pair, number):
        first, second = gather[pair]
        if number == 0:
            for copy in hcopies[pair]:
                copy.wait_recv()
            for ring in first:
                ring.start()
        elif number == 1:
            for ring in first:
                ring.forward()
        elif number == 2:
            for ring in first:
                ring.finish()
            for ring in second:
                ring.start()
        elif number == 3:
            for ring in second:
                ring.forward()
        else:
            for ring in second:
                ring.finish()

    def output(pair):
        mine = ag[pair]

        def pick(q, carry):
            owner = owner_ref[q]
            for h in range(2):
                rows = mine[h, lax.div(owner, 4), lax.rem(owner, 4)]
                for c in range(8):
                    lhs[pl.ds(pl.multiple_of(q * 32 + h * 16, 16), 16), c * WIDE : (c + 1) * WIDE] = rows[c]
            return carry

        lax.fori_loop(0, 16, pick, 0)

        def block(i, carry):
            rows = pl.ds(pl.multiple_of(i * 256, 256), 256)
            out = jnp.dot(
                lhs[rows, :],
                wo[:, pair * WIDE : (pair + 1) * WIDE, :].reshape(8 * WIDE, 448),
                preferred_element_type=F32,
            )
            oacc[rows, :] = out if pair == 0 else oacc[rows, :] + out
            return carry

        lax.fori_loop(0, 2, block, 0)

    pump(3)
    multiply(0)
    multiply(1)
    pump(4)
    multiply(2)
    total(0)
    cached(0, 0, BLOCKS // 2)
    oring.forward()
    across_out(z)
    across_out(lax.rem(z + 3, 4))
    across_out(lax.rem(z + 1, 4))
    pump(5)
    multiply(3)
    total(1)
    cached(0, BLOCKS // 2, BLOCKS)
    pump(6)
    multiply(4)
    oring.finish()
    across_out(lax.rem(z + 2, 4))
    total(2)
    total(3)
    cached(1, 0, BLOCKS // 2)
    pump(7)
    multiply(5)
    total(4)
    fresh(0)
    share(0)
    cached(1, BLOCKS // 2, BLOCKS)
    pump(8)
    multiply(6)
    stage(0, 0)
    total(5)
    cached(2, 0, BLOCKS // 2)
    multiply(7)
    total(6)
    fresh(1)
    share(1)
    stage(0, 1)
    multiply(8)
    stage(0, 2)
    total(7)
    stage(1, 0)
    cached(2, BLOCKS // 2, BLOCKS)
    stage(1, 1)
    stage(0, 3)
    total(8)
    fresh(2)
    share(2)
    stage(1, 2)
    stage(2, 0)
    stage(0, 4)
    for copy in ocopies:
        copy.wait_recv()
    stage(2, 1)
    output(0)
    stage(2, 2)
    stage(1, 3)
    stage(1, 4)
    output(1)
    stage(2, 3)
    stage(2, 4)
    output(2)

    home = lax.div(row, 2)
    which = lax.rem(row, 2)

    def last(q):
        return pltpu.make_async_remote_copy(
            src_ref=fsend.at[q],
            dst_ref=frecv.at[which, col],
            send_sem=fs.at[q],
            recv_sem=fr.at[which, col],
            device_id=(q, home),
            device_id_type=MESH,
        )

    def stays(q):
        return jnp.logical_and(q == row, home == col)

    def hand(q, carry):
        fsend[q] = oacc[pl.ds(pl.multiple_of(q * 32, 32), 32), :].astype(BF16)

        @pl.when(jnp.logical_not(stays(q)))
        def _():
            last(q).start()

        @pl.when(stays(q))
        def _():
            frecv[which, col] = fsend[q]

        return carry

    lax.fori_loop(0, 16, hand, 0)
    rcopy.wait()
    for k in range(2):
        for c in range(8):

            @pl.when(jnp.logical_not(jnp.logical_and(2 * col + k == row, col == c)))
            def _():
                pltpu.make_async_remote_copy(
                    src_ref=fsend.at[0], dst_ref=frecv.at[k, c], send_sem=fs.at[0],
                    recv_sem=fr.at[k, c], device_id=(2 * col + k, c), device_id_type=MESH,
                ).wait_recv()

        lanes = slice(k * 448, (k + 1) * 448)
        out_ref[:, lanes] = (
            frecv[k].reshape(256, 448).astype(F32) + bo_ref[...][:, lanes] + res[...][:, lanes].astype(F32)
        ).astype(BF16)

    def sent(q, carry):
        @pl.when(jnp.logical_not(stays(q)))
        def _():
            last(q).wait_send()

        return carry

    lax.fori_loop(0, 16, sent, 0)
    for copy in xcopies + ccopies + ocopies + sum(hcopies, []):
        copy.wait_send()
    for ring in [yring, zring, oring] + wring + [r for g in gather for rs in g for r in rs]:
        ring.drain()
    for part in range(PARTS):
        for i in range(3):
            arrived(part, i).wait_send()


def layer(owner_slot, lengths, hidden, gain, shift, wq, wkv, bq, bkv, cache_k, cache_v, w_out, bo):
    dma = pltpu.SemaphoreType.DMA
    vmem = pl.BlockSpec(memory_space=pltpu.VMEM)
    smem = pl.BlockSpec(memory_space=pltpu.SMEM)
    hbm = pl.BlockSpec(memory_space=pl.ANY)
    out = jax.ShapeDtypeStruct((256, 768), BF16)
    return pl.pallas_call(
        layer_kernel,
        out_shape=(jax.ShapeDtypeStruct((256, 896), BF16), out, out),
        in_specs=[smem, smem, hbm, vmem, vmem, hbm, hbm, vmem, vmem, hbm, hbm, hbm, vmem],
        out_specs=(vmem, vmem, vmem),
        scratch_shapes=[
            pltpu.VMEM((32, 7168), BF16),
            pltpu.VMEM((4, 32, 1792), BF16),
            pltpu.VMEM((4, 4, 32, 1792), BF16),
            pltpu.VMEM((4, 8, 32, 1792), BF16),
            pltpu.VMEM((PARTS, 4, 448, WIDE), BF16),
            pltpu.VMEM((PARTS, 3, 256, WIDE), BF16),
            pltpu.VMEM((PARTS, 3, 256, WIDE), BF16),
            pltpu.VMEM((PARTS, 256, WIDE), F32),
            pltpu.VMEM((3, 256, WIDE), BF16),
            pltpu.VMEM((2, KEYS, WIDE), BF16),
            pltpu.VMEM((2, KEYS, WIDE), BF16),
            pltpu.VMEM((6, 256, 1), F32),
            pltpu.VMEM((6, 256, 1), F32),
            pltpu.VMEM((6, 256, HEAD), F32),
            pltpu.VMEM((3, 8, 2, 16, WIDE), BF16),
            pltpu.VMEM((2, 4, 4, 8, 16, WIDE), BF16),
            pltpu.VMEM((2, 4, 4, 8, 16, WIDE), BF16),
            pltpu.VMEM((2, 4, 4, 8, 16, WIDE), BF16),
            pltpu.VMEM((8, 768, 448), BF16),
            pltpu.VMEM((512, 8 * WIDE), BF16),
            pltpu.VMEM((512, 448), F32),
            pltpu.VMEM((16, 32, 448), BF16),
            pltpu.VMEM((2, 8, 32, 448), BF16),
            pltpu.VMEM((256, 896), BF16),
            dma,
            dma((PARTS,)),
            dma((2,)), dma((2,)),
            dma((3,)), dma((3,)),
            dma((4,)), dma((4,)),
            dma((4,)), dma((4,)),
            dma((4,)), dma((4,)),
            dma((PARTS, 4)), dma((PARTS, 4)),
            dma((PARTS, 3)), dma((PARTS, 3)),
            dma, dma,
            dma((4,)), dma((4,)),
            dma((4,)), dma((4,)),
            dma((3, 7)), dma((3, 7)),
            dma((3, 2, 2, 4)), dma((3, 2, 2, 4)),
            dma((16,)), dma((2, 8)),
        ],
        compiler_params=pltpu.CompilerParams(
            collective_id=0, has_side_effects=True, vmem_limit_bytes=67_000_000
        ),
        name="layer",
    )(owner_slot, lengths, hidden, gain, shift, wq, wkv, bq, bkv, cache_k, cache_v, w_out, bo)


def local(
    hidden_in, norm_gain, norm_bias, w_query, w_keyval, bias_query, bias_keyval,
    cache_keys, cache_values, cache_lengths, owner_slot, w_out, bias_out,
):
    hidden_out, new_k, new_v = layer(
        owner_slot, cache_lengths, hidden_in, norm_gain[None], norm_bias[None],
        w_query, w_keyval.transpose(1, 0, 2), bias_query[None], bias_keyval,
        cache_keys[0], cache_values[0], w_out, bias_out[None],
    )
    return (hidden_out, new_k[None], new_v[None])


def solution(mesh):
    placed = (
        P("row", None), P(), P(), P("row", "col"), P("row", None, "col"), P("col"), P(None, "col"),
        P("row", None, "col"), P("row", None, "col"), P(), P(), P("col", "row"), P("col"),
    )
    return jax.shard_map(
        local,
        mesh=mesh,
        in_specs=placed,
        out_specs=(P("row", "col"), P("row", None, "col"), P("row", None, "col")),
        check_vma=False,
    )
```

```python
import jax
import jax.numpy as jnp
from jax import lax
from jax.experimental import pallas as pl
from jax.experimental.pallas import tpu as pltpu
from jax.sharding import PartitionSpec as P

HEAD = 128
MESH = pl.DeviceIdType.MESH
BF16 = jnp.bfloat16
F32 = jnp.float32
NEG = -1e30


def place():
    row, col = lax.axis_index("row"), lax.axis_index("col")
    return row, col, lax.div(row, 4), lax.rem(row, 4), lax.div(col, 2), lax.rem(col, 2)


def send(src, dst, send_sem, recv_sem, row, col):
    copy = pltpu.make_async_remote_copy(
        src_ref=src,
        dst_ref=dst,
        send_sem=send_sem,
        recv_sem=recv_sem,
        device_id=(row, col),
        device_id_type=MESH,
    )
    copy.start()
    return copy


def greet(peers):
    barrier = pltpu.get_barrier_semaphore()
    for row, col in peers:
        pl.semaphore_signal(barrier, inc=1, device_id=(row, col), device_id_type=MESH)
    pl.semaphore_wait(barrier, len(peers))


class Ring:
    def __init__(self, me, device, block, half, send_sem, recv_sem):
        self.me, self.device, self.block, self.half = me, device, block, half
        self.send_sem, self.recv_sem = send_sem, recv_sem
        self.copies = []

    def start(self):
        for i, step in enumerate((1, 3)):
            to = self.device(lax.rem(self.me + step, 4))
            view = self.block(self.me)
            self.copies.append(send(view, view, self.send_sem(i), self.recv_sem(i), *to))

    def forward(self):
        for i, step in enumerate((1, 3)):
            self.copies[i].wait_recv()
            to = self.device(lax.rem(self.me + step, 4))
            view = self.half(lax.rem(self.me + 4 - step, 4), i)
            self.copies.append(send(view, view, self.send_sem(2 + i), self.recv_sem(2 + i), *to))

    def finish(self):
        for copy in self.copies[2:]:
            copy.wait_recv()

    def drain(self):
        for copy in self.copies:
            copy.wait_send()


ORDER = ((0, 0), (1, 0), (2, 0), (0, 1), (0, 2), (1, 1), (2, 1), (1, 2), (2, 2))
PARTS = len(ORDER)
WIDE = 256
KEYS = 1024
HEAVY = 0
BLOCKS = 4096 // KEYS


def layer_kernel(
    owner_ref, len_ref, hid_ref, gain_ref, shift_ref, wq_ref, wkv_ref, bq_ref, bkv_ref, ck_ref, cv_ref,
    wout_ref, bo_ref,
    out_ref, k_ref, v_ref,
    hbuf, act, ybuf, abuf, wbuf, psend, rbuf, acc, qbuf, kbuf, vbuf, m_s, l_s, o_s,
    asend, ag0, ag1, ag2, wo, lhs, oacc, fsend, frecv, res, wraw,
    hsem, lsem, ksem, vsem, xs, xr, ys, yr, zs, zr, cs, cr, ws, wr, ps, pr,
    osem, rsem, os_, or_, ocs, ocr, hs, hr, gs, gr, fs, fr,
):
    row, col, y, x, z, core = place()
    at = lambda yy, xx: yy * 4 + xx
    other = z * 2 + (1 - core)
    peers = [(at(y, lax.rem(x + d, 4)), col) for d in (1, 2, 3)]
    peers += [(at(lax.rem(y + d, 4), x), col) for d in (1, 3)]
    peers += [(row, lax.rem(z + d, 4) * 2 + core) for d in (1, 3)]
    peers += [(row, other)]

    def request_of(slot):
        request = 0
        for i in range(16):
            request = jnp.where(owner_ref[i] == slot, i, request)
        return request

    hcopy = pltpu.make_async_copy(hid_ref.at[pl.ds(col * 32, 32)], hbuf, hsem)
    hcopy.start()
    local = []
    for p in range(PARTS):
        kind, pair = ORDER[p]
        lanes = pl.ds(pair * WIDE, WIDE)
        source = wq_ref.at[:, lanes] if kind == 0 else wkv_ref.at[kind - 1, :, lanes]
        local.append(pltpu.make_async_copy(source, wbuf.at[p, y], lsem.at[p]))
        local[p].start()

    def fetch(n):
        pair, block, slot = lax.div(n, BLOCKS), lax.rem(n, BLOCKS), lax.rem(n, 2)
        place_of = (pl.ds(block * KEYS, KEYS), pl.ds(pl.multiple_of(pair * WIDE, WIDE), WIDE))
        return (
            pltpu.make_async_copy(ck_ref.at[place_of], kbuf.at[slot], ksem.at[slot]),
            pltpu.make_async_copy(cv_ref.at[place_of], vbuf.at[slot], vsem.at[slot]),
        )

    for copy in fetch(jnp.int32(0)):
        copy.start()
    ocopy = pltpu.make_async_copy(wout_ref, wraw, osem)
    ocopy.start()
    rcopy = pltpu.make_async_copy(hid_ref.at[:, pl.ds(pl.multiple_of(col * 896, 128), 896)], res, rsem)
    rcopy.start()
    greet(peers)

    wring = [
        Ring(
            y,
            lambda o: (at(o, x), col),
            lambda o, p=p: wbuf.at[p, o],
            lambda o, i, p=p: wbuf.at[p, o, pl.ds(224 * i, 224)],
            lambda i, p=p: ws.at[p, i],
            lambda i, p=p: wr.at[p, i],
        )
        for p in range(PARTS)
    ]

    def launch(p):
        local[p].wait()
        wring[p].start()

    def pump(p):
        wring[p].forward()

    launch(0)
    launch(1)
    launch(2)
    hcopy.wait()
    inputs = hbuf[...].astype(F32)
    width = inputs.shape[1]
    centered = inputs - jnp.sum(inputs, axis=1, keepdims=True) * (1.0 / width)
    var = jnp.sum(centered * centered, axis=1, keepdims=True) * (1.0 / width)
    normed = (centered * lax.rsqrt(var + 1e-05) * gain_ref[...][None] + shift_ref[...][None]).astype(BF16)
    for xx in range(4):
        for yy in range(4):
            begin = (yy * 4 + xx) * 448
            act[xx, :, yy * 448 : (yy + 1) * 448] = normed[:, begin : begin + 448]
    pump(0)
    xcopies = []
    for d in (1, 2, 3):
        to = lax.rem(x + d, 4)
        xcopies.append(
            send(act.at[to], ybuf.at[y, x], xs.at[d - 1], xr.at[d - 1], at(y, to), col)
        )
    ybuf[y, x] = act[x]
    ocopy.wait()
    wo[col] = wraw[...].T
    for copy in xcopies:
        copy.wait_recv()
    yring = Ring(
        y,
        lambda o: (at(o, x), col),
        lambda o: ybuf.at[o],
        lambda o, i: ybuf.at[o, pl.ds(2 * i, 2)],
        lambda i: ys.at[i],
        lambda i: yr.at[i],
    )
    yring.start()
    pump(1)
    yring.forward()
    pump(2)
    launch(3)
    yring.finish()
    for s in range(4):
        request = request_of(y * 4 + s)
        abuf[s, col] = ybuf[lax.div(request, 4), lax.rem(request, 4)]
    zring = Ring(
        z,
        lambda o: (row, o * 2 + core),
        lambda o: abuf.at[:, o * 2 + core],
        lambda o, i: abuf.at[pl.ds(2 * i, 2), o * 2 + core],
        lambda i: zs.at[i],
        lambda i: zr.at[i],
    )
    zring.start()
    ccopies = []

    def across(view):
        i = len(ccopies)
        ccopies.append(send(view, view, cs.at[i], cr.at[i], row, other))

    across(zring.block(z))
    launch(4)
    pump(3)
    zring.forward()
    across(zring.block(lax.rem(z + 3, 4)))
    across(zring.block(lax.rem(z + 1, 4)))
    launch(5)
    pump(4)
    zring.finish()
    across(zring.block(lax.rem(z + 2, 4)))
    oring = Ring(
        z,
        lambda o: (row, o * 2 + core),
        lambda o: wo.at[o * 2 + core],
        lambda o, i: wo.at[o * 2 + core, pl.ds(384 * i, 384)],
        lambda i: os_.at[i],
        lambda i: or_.at[i],
    )
    oring.start()
    ocopies = []

    def across_out(o):
        i, view = len(ocopies), oring.block(o)
        ocopies.append(send(view, view, ocs.at[i], ocr.at[i], row, other))

    for copy in ccopies:
        copy.wait_recv()

    def multiply(part):
        wring[part].finish()

        def block(i, carry):
            to = lax.rem(x + i + 1, 4)
            out = jnp.dot(
                abuf[to].reshape(256, 1792),
                wbuf[part].reshape(1792, WIDE),
                preferred_element_type=F32,
            )
            acc[part] = out

            @pl.when(i < 3)
            def _():
                psend[part, i] = out.astype(BF16)
                send(
                    psend.at[part, i], rbuf.at[part, i], ps.at[part, i], pr.at[part, i],
                    at(y, to), col,
                )

            return carry

        lax.fori_loop(0, 4, block, 0)

    def arrived(part, i):
        return pltpu.make_async_remote_copy(
            src_ref=psend.at[part, i],
            dst_ref=rbuf.at[part, i],
            send_sem=ps.at[part, i],
            recv_sem=pr.at[part, i],
            device_id=(at(y, lax.rem(x + i + 1, 4)), col),
            device_id_type=MESH,
        )

    def total(part):
        for i in range(3):
            arrived(part, i).wait_recv()
        out = acc[part]
        for i in range(3):
            out = out + rbuf[part, i].astype(F32)
        kind, pair = ORDER[part]
        lanes = slice(pair * WIDE, (pair + 1) * WIDE)
        if kind == 0:
            qbuf[pair] = ((out + bq_ref[lanes][None]) * (HEAD**-0.5)).astype(BF16)
        else:
            to_ref = (k_ref, v_ref)[kind - 1]
            to_ref[:, lanes] = (out + bkv_ref[kind - 1 : kind, lanes]).astype(BF16)

    m_s[...] = jnp.full_like(m_s, NEG)
    l_s[...] = jnp.zeros_like(l_s)
    o_s[...] = jnp.zeros_like(o_s)
    length = len_ref[request_of(row)]

    def visit(pair, keys, values, bias):
        for j in range(2):
            h = pair * 2 + j
            lanes = slice(j * HEAD, (j + 1) * HEAD)
            scores = lax.dot_general(
                qbuf[pair, :, lanes], keys[:, lanes], (((1,), (1,)), ((), ())),
                preferred_element_type=F32,
            )
            scores = scores + bias
            old = m_s[h]
            new = jnp.maximum(old, jnp.max(scores, axis=1, keepdims=True))
            probs = jnp.exp(scores - new)
            factor = jnp.exp(old - new)
            m_s[h] = new
            l_s[h] = l_s[h] * factor + jnp.sum(probs, axis=1, keepdims=True)
            o_s[h] = o_s[h] * factor + jnp.dot(
                probs.astype(BF16), values[:, lanes], preferred_element_type=F32
            )

    def cached(pair, begin, end):
        def step(block, carry):
            n = pair * BLOCKS + block
            slot = lax.rem(n, 2)
            for copy in fetch(n):
                copy.wait()

            @pl.when(n + 1 < 3 * BLOCKS)
            def _():
                for copy in fetch(n + 1):
                    copy.start()

            pos = block * KEYS + lax.broadcasted_iota(jnp.int32, (1, KEYS), 1)
            visit(pair, kbuf[slot], vbuf[slot], jnp.where(pos < length, 0.0, NEG))
            return carry

        lax.fori_loop(begin, end, step, 0)

    late = lax.broadcasted_iota(jnp.int32, (256, 256), 1) > lax.broadcasted_iota(
        jnp.int32, (256, 256), 0
    )
    causal = jnp.where(late, NEG, 0.0)

    def fresh(pair):
        lanes = slice(pair * WIDE, (pair + 1) * WIDE)
        visit(pair, k_ref[:, lanes], v_ref[:, lanes], causal)
        for j in range(2):
            h = pair * 2 + j
            done = (o_s[h] / l_s[h]).astype(BF16)
            asend[pair, :, :, :, j * HEAD : (j + 1) * HEAD] = done.reshape(8, 2, 16, HEAD)

    ag = (ag0, ag1, ag2)
    hcopies = [[], [], []]

    def share(pair):
        mine = ag[pair]
        for d in range(1, 8):
            to = lax.rem(col + d, 8)
            hcopies[pair].append(
                send(asend.at[pair, to], mine.at[:, y, x, col], hs.at[pair, d - 1], hr.at[pair, d - 1],
                     row, to)
            )
        mine[:, y, x, col] = asend[pair, col]

    xline = lambda o: (at(y, o), col)
    yline = lambda o: (at(o, x), col)

    def rings(pair):
        mine = ag[pair]

        def sems(phase, k):
            return (lambda i: gs.at[pair, phase, k, i]), (lambda i: gr.at[pair, phase, k, i])

        if pair < HEAVY:
            return (
                [Ring(y, yline, lambda o: mine.at[:, o, x], lambda o, i: mine.at[i, o, x], *sems(0, 0))],
                [Ring(x, xline, lambda o: mine.at[:, :, o], lambda o, i: mine.at[i, :, o], *sems(1, 0))],
            )
        return (
            [
                Ring(x, xline, lambda o: mine.at[0, y, o],
                     lambda o, i: mine.at[0, y, o, pl.ds(4 * i, 4)], *sems(0, 0)),
                Ring(y, yline, lambda o: mine.at[1, o, x],
                     lambda o, i: mine.at[1, o, x, pl.ds(4 * i, 4)], *sems(0, 1)),
            ],
            [
                Ring(y, yline, lambda o: mine.at[0, o],
                     lambda o, i: mine.at[0, o, pl.ds(2 * i, 2)], *sems(1, 0)),
                Ring(x, xline, lambda o: mine.at[1, :, o],
                     lambda o, i: mine.at[1, pl.ds(2 * i, 2), o], *sems(1, 1)),
            ],
        )

    gather = [rings(pair) for pair in range(3)]

    def stage(pair, number):
        first, second = gather[pair]
        if number == 0:
            for copy in hcopies[pair]:
                copy.wait_recv()
            for ring in first:
                ring.start()
        elif number == 1:
            for ring in first:
                ring.forward()
        elif number == 2:
            for ring in first:
                ring.finish()
            for ring in second:
                ring.start()
        elif number == 3:
            for ring in second:
                ring.forward()
        else:
            for ring in second:
                ring.finish()

    def output(pair):
        mine = ag[pair]

        def pick(q, carry):
            owner = owner_ref[q]
            for h in range(2):
                rows = mine[h, lax.div(owner, 4), lax.rem(owner, 4)]
                for c in range(8):
                    lhs[pl.ds(pl.multiple_of(q * 32 + h * 16, 16), 16), c * WIDE : (c + 1) * WIDE] = rows[c]
            return carry

        lax.fori_loop(0, 16, pick, 0)

        def block(i, carry):
            rows = pl.ds(pl.multiple_of(i * 256, 256), 256)
            out = jnp.dot(
                lhs[rows, :],
                wo[:, pair * WIDE : (pair + 1) * WIDE, :].reshape(8 * WIDE, 448),
                preferred_element_type=F32,
            )
            oacc[rows, :] = out if pair == 0 else oacc[rows, :] + out
            return carry

        lax.fori_loop(0, 2, block, 0)

    multiply(0)
    launch(6)
    pump(5)
    multiply(1)
    multiply(2)
    launch(7)
    total(0)
    cached(0, 0, BLOCKS // 2)
    pump(6)
    launch(8)
    multiply(3)
    oring.forward()
    across_out(z)
    across_out(lax.rem(z + 3, 4))
    across_out(lax.rem(z + 1, 4))
    cached(0, BLOCKS // 2, BLOCKS)
    pump(7)
    multiply(4)
    total(1)
    total(2)
    fresh(0)
    share(0)
    total(3)
    cached(1, 0, BLOCKS // 2)
    pump(8)
    multiply(5)
    cached(1, BLOCKS // 2, BLOCKS)
    multiply(6)
    oring.finish()
    across_out(lax.rem(z + 2, 4))
    total(4)
    cached(2, 0, BLOCKS // 2)
    multiply(7)
    total(5)
    total(6)
    fresh(1)
    share(1)
    multiply(8)
    stage(0, 0)
    stage(1, 0)
    cached(2, BLOCKS // 2, BLOCKS)
    stage(0, 1)
    stage(1, 1)
    total(7)
    stage(0, 2)
    total(8)
    fresh(2)
    share(2)
    stage(1, 2)
    stage(0, 3)
    stage(2, 0)
    stage(2, 1)
    for copy in ocopies:
        copy.wait_recv()
    stage(1, 3)
    stage(2, 2)
    stage(0, 4)
    output(0)
    stage(1, 4)
    output(1)
    stage(2, 3)
    stage(2, 4)
    output(2)

    home = lax.div(row, 2)
    which = lax.rem(row, 2)

    def last(q):
        return pltpu.make_async_remote_copy(
            src_ref=fsend.at[q],
            dst_ref=frecv.at[which, col],
            send_sem=fs.at[q],
            recv_sem=fr.at[which, col],
            device_id=(q, home),
            device_id_type=MESH,
        )

    def stays(q):
        return jnp.logical_and(q == row, home == col)

    def hand(q, carry):
        fsend[q] = oacc[pl.ds(pl.multiple_of(q * 32, 32), 32), :].astype(BF16)

        @pl.when(jnp.logical_not(stays(q)))
        def _():
            last(q).start()

        @pl.when(stays(q))
        def _():
            frecv[which, col] = fsend[q]

        return carry

    lax.fori_loop(0, 16, hand, 0)
    rcopy.wait()
    for k in range(2):
        for c in range(8):

            @pl.when(jnp.logical_not(jnp.logical_and(2 * col + k == row, col == c)))
            def _():
                pltpu.make_async_remote_copy(
                    src_ref=fsend.at[0], dst_ref=frecv.at[k, c], send_sem=fs.at[0],
                    recv_sem=fr.at[k, c], device_id=(2 * col + k, c), device_id_type=MESH,
                ).wait_recv()

        lanes = slice(k * 448, (k + 1) * 448)
        out_ref[:, lanes] = (
            frecv[k].reshape(256, 448).astype(F32) + bo_ref[lanes][None] + res[...][:, lanes].astype(F32)
        ).astype(BF16)

    def sent(q, carry):
        @pl.when(jnp.logical_not(stays(q)))
        def _():
            last(q).wait_send()

        return carry

    lax.fori_loop(0, 16, sent, 0)
    for copy in xcopies + ccopies + ocopies + sum(hcopies, []):
        copy.wait_send()
    for ring in [yring, zring, oring] + wring + [r for g in gather for rs in g for r in rs]:
        ring.drain()
    for part in range(PARTS):
        for i in range(3):
            arrived(part, i).wait_send()


def layer(owner_slot, lengths, hidden, gain, shift, wq, wkv, bq, bkv, cache_k, cache_v, w_out, bo):
    dma = pltpu.SemaphoreType.DMA
    vmem = pl.BlockSpec(memory_space=pltpu.VMEM)
    smem = pl.BlockSpec(memory_space=pltpu.SMEM)
    hbm = pl.BlockSpec(memory_space=pl.ANY)
    out = jax.ShapeDtypeStruct((256, 768), BF16)
    return pl.pallas_call(
        layer_kernel,
        out_shape=(jax.ShapeDtypeStruct((256, 896), BF16), out, out),
        in_specs=[smem, smem, hbm, vmem, vmem, hbm, hbm, vmem, vmem, hbm, hbm, hbm, vmem],
        out_specs=(vmem, vmem, vmem),
        scratch_shapes=[
            pltpu.VMEM((32, 7168), BF16),
            pltpu.VMEM((4, 32, 1792), BF16),
            pltpu.VMEM((4, 4, 32, 1792), BF16),
            pltpu.VMEM((4, 8, 32, 1792), BF16),
            pltpu.VMEM((PARTS, 4, 448, WIDE), BF16),
            pltpu.VMEM((PARTS, 3, 256, WIDE), BF16),
            pltpu.VMEM((PARTS, 3, 256, WIDE), BF16),
            pltpu.VMEM((PARTS, 256, WIDE), F32),
            pltpu.VMEM((3, 256, WIDE), BF16),
            pltpu.VMEM((2, KEYS, WIDE), BF16),
            pltpu.VMEM((2, KEYS, WIDE), BF16),
            pltpu.VMEM((6, 256, 1), F32),
            pltpu.VMEM((6, 256, 1), F32),
            pltpu.VMEM((6, 256, HEAD), F32),
            pltpu.VMEM((3, 8, 2, 16, WIDE), BF16),
            pltpu.VMEM((2, 4, 4, 8, 16, WIDE), BF16),
            pltpu.VMEM((2, 4, 4, 8, 16, WIDE), BF16),
            pltpu.VMEM((2, 4, 4, 8, 16, WIDE), BF16),
            pltpu.VMEM((8, 768, 448), BF16),
            pltpu.VMEM((512, 8 * WIDE), BF16),
            pltpu.VMEM((512, 448), F32),
            pltpu.VMEM((16, 32, 448), BF16),
            pltpu.VMEM((2, 8, 32, 448), BF16),
            pltpu.VMEM((256, 896), BF16),
            pltpu.VMEM((448, 768), BF16),
            dma,
            dma((PARTS,)),
            dma((2,)), dma((2,)),
            dma((3,)), dma((3,)),
            dma((4,)), dma((4,)),
            dma((4,)), dma((4,)),
            dma((4,)), dma((4,)),
            dma((PARTS, 4)), dma((PARTS, 4)),
            dma((PARTS, 3)), dma((PARTS, 3)),
            dma, dma,
            dma((4,)), dma((4,)),
            dma((4,)), dma((4,)),
            dma((3, 7)), dma((3, 7)),
            dma((3, 2, 2, 4)), dma((3, 2, 2, 4)),
            dma((16,)), dma((2, 8)),
        ],
        compiler_params=pltpu.CompilerParams(
            collective_id=0, has_side_effects=True, vmem_limit_bytes=58 * 2**20
        ),
        name="layer",
    )(owner_slot, lengths, hidden, gain, shift, wq, wkv, bq, bkv, cache_k, cache_v, w_out, bo)


def settle_kernel(a_ref, b_ref, c_ref, a_out, b_out, c_out):
    a_out[...] = a_ref[...]
    b_out[...] = b_ref[...]
    c_out[...] = c_ref[...]


def settle(*arrays):
    def half(a):
        return pl.BlockSpec((a.shape[0] // 2, a.shape[1]), lambda i: (i, 0))

    return pl.pallas_call(
        settle_kernel,
        out_shape=tuple(jax.ShapeDtypeStruct(a.shape, a.dtype) for a in arrays),
        grid=(2,),
        in_specs=[half(a) for a in arrays],
        out_specs=tuple(half(a) for a in arrays),
        name="settle",
    )(*arrays)


def local(
    hidden_in, norm_gain, norm_bias, w_query, w_keyval, bias_query, bias_keyval,
    cache_keys, cache_values, cache_lengths, owner_slot, w_out, bias_out,
):
    hidden_out, new_k, new_v = layer(
        owner_slot, cache_lengths, hidden_in, norm_gain, norm_bias,
        w_query, w_keyval.transpose(1, 0, 2), bias_query, bias_keyval,
        cache_keys[0], cache_values[0], w_out.T, bias_out,
    )
    hidden_out, new_k, new_v = settle(hidden_out, new_k, new_v)
    return (hidden_out, new_k[None], new_v[None])


def solution(mesh):
    placed = (
        P("row", None), P(), P(), P("row", "col"), P("row", None, "col"), P("col"), P(None, "col"),
        P("row", None, "col"), P("row", None, "col"), P(), P(), P("col", "row"), P("col"),
    )
    return jax.shard_map(
        local,
        mesh=mesh,
        in_specs=placed,
        out_specs=(P("row", "col"), P("row", None, "col"), P("row", None, "col")),
        check_vma=False,
    )
```

```python
import jax
import jax.numpy as jnp
from jax import lax
from jax.experimental import pallas as pl
from jax.experimental.pallas import tpu as pltpu
from jax.sharding import PartitionSpec as P

HEAD = 128
MESH = pl.DeviceIdType.MESH
BF16 = jnp.bfloat16
F32 = jnp.float32
NEG = -1e30


def place():
    row, col = lax.axis_index("row"), lax.axis_index("col")
    return row, col, lax.div(row, 4), lax.rem(row, 4), lax.div(col, 2), lax.rem(col, 2)


def send(src, dst, send_sem, recv_sem, row, col):
    copy = pltpu.make_async_remote_copy(
        src_ref=src,
        dst_ref=dst,
        send_sem=send_sem,
        recv_sem=recv_sem,
        device_id=(row, col),
        device_id_type=MESH,
    )
    copy.start()
    return copy


def greet(peers):
    barrier = pltpu.get_barrier_semaphore()
    for row, col in peers:
        pl.semaphore_signal(barrier, inc=1, device_id=(row, col), device_id_type=MESH)
    pl.semaphore_wait(barrier, len(peers))


class Ring:
    def __init__(self, me, device, block, half, send_sem, recv_sem):
        self.me, self.device, self.block, self.half = me, device, block, half
        self.send_sem, self.recv_sem = send_sem, recv_sem
        self.copies = []

    def start(self):
        for i, step in enumerate((1, 3)):
            to = self.device(lax.rem(self.me + step, 4))
            view = self.block(self.me)
            self.copies.append(send(view, view, self.send_sem(i), self.recv_sem(i), *to))

    def forward(self):
        for i, step in enumerate((1, 3)):
            self.copies[i].wait_recv()
            to = self.device(lax.rem(self.me + step, 4))
            view = self.half(lax.rem(self.me + 4 - step, 4), i)
            self.copies.append(send(view, view, self.send_sem(2 + i), self.recv_sem(2 + i), *to))

    def finish(self):
        for copy in self.copies[2:]:
            copy.wait_recv()

    def drain(self):
        for copy in self.copies:
            copy.wait_send()


ORDER = ((0, 0), (0, 1), (1, 0), (2, 0), (0, 2), (1, 1), (2, 1), (1, 2), (2, 2))
PARTS = len(ORDER)
WIDE = 256
KEYS = 1024
HEAVY = 0
BLOCKS = 4096 // KEYS


def layer_kernel(
    owner_ref, len_ref, hid_ref, gain_ref, shift_ref, wq_ref, wkv_ref, bq_ref, bkv_ref, ck_ref, cv_ref,
    wout_ref, bo_ref,
    out_ref, k_ref, v_ref,
    hbuf, act, ybuf, abuf, wbuf, psend, rbuf, acc, qbuf, kbuf, vbuf, m_s, l_s, o_s,
    asend, ag0, ag1, ag2, wo, lhs, oacc, fsend, frecv, res, wraw, kvraw,
    hsem, lsem, ksem, vsem, xs, xr, ys, yr, zs, zr, cs, cr, ws, wr, ps, pr,
    osem, rsem, os_, or_, ocs, ocr, hs, hr, gs, gr, fs, fr,
):
    row, col, y, x, z, core = place()
    at = lambda yy, xx: yy * 4 + xx
    other = z * 2 + (1 - core)
    peers = [(at(y, lax.rem(x + d, 4)), col) for d in (1, 2, 3)]
    peers += [(at(lax.rem(y + d, 4), x), col) for d in (1, 3)]
    peers += [(row, lax.rem(z + d, 4) * 2 + core) for d in (1, 3)]
    peers += [(row, other)]

    def request_of(slot):
        request = 0
        for i in range(16):
            request = jnp.where(owner_ref[i] == slot, i, request)
        return request

    hcopy = pltpu.make_async_copy(hid_ref.at[pl.ds(col * 32, 32)], hbuf, hsem)
    hcopy.start()
    local = {}
    for p in range(PARTS):
        kind, pair = ORDER[p]
        lanes = pl.ds(pair * WIDE, WIDE)
        if kind == 0:
            local[p] = pltpu.make_async_copy(wq_ref.at[:, lanes], wbuf.at[p, y], lsem.at[p])
            local[p].start()

    def fetch(n):
        pair, block, slot = lax.div(n, BLOCKS), lax.rem(n, BLOCKS), lax.rem(n, 2)
        place_of = (pl.ds(block * KEYS, KEYS), pl.ds(pl.multiple_of(pair * WIDE, WIDE), WIDE))
        return (
            pltpu.make_async_copy(ck_ref.at[place_of], kbuf.at[slot], ksem.at[slot]),
            pltpu.make_async_copy(cv_ref.at[place_of], vbuf.at[slot], vsem.at[slot]),
        )

    kvcopy = pltpu.make_async_copy(wkv_ref, kvraw, lsem.at[2])
    kvcopy.start()
    for copy in fetch(jnp.int32(0)):
        copy.start()
    ocopy = pltpu.make_async_copy(wout_ref, wraw, osem)
    ocopy.start()
    rcopy = pltpu.make_async_copy(hid_ref.at[:, pl.ds(pl.multiple_of(col * 896, 128), 896)], res, rsem)
    rcopy.start()
    greet(peers)

    wring = [
        Ring(
            y,
            lambda o: (at(o, x), col),
            lambda o, p=p: wbuf.at[p, o],
            lambda o, i, p=p: wbuf.at[p, o, pl.ds(224 * i, 224)],
            lambda i, p=p: ws.at[p, i],
            lambda i, p=p: wr.at[p, i],
        )
        for p in range(PARTS)
    ]

    def launch(p):
        if p in local:
            local[p].wait()
        wring[p].start()

    def pump(p):
        wring[p].forward()

    def untangle(parts):
        for p in parts:
            kind, pair = ORDER[p]
            wbuf[p, y] = kvraw[:, kind - 1, pair * WIDE : (pair + 1) * WIDE]

    launch(0)
    launch(1)
    hcopy.wait()
    inputs = hbuf[...].astype(F32)
    width = inputs.shape[1]
    centered = inputs - jnp.sum(inputs, axis=1, keepdims=True) * (1.0 / width)
    var = jnp.sum(centered * centered, axis=1, keepdims=True) * (1.0 / width)
    normed = (centered * lax.rsqrt(var + 1e-05) * gain_ref[...][None] + shift_ref[...][None]).astype(BF16)
    for xx in range(4):
        for yy in range(4):
            begin = (yy * 4 + xx) * 448
            act[xx, :, yy * 448 : (yy + 1) * 448] = normed[:, begin : begin + 448]
    pump(0)
    xcopies = []
    for d in (1, 2, 3):
        to = lax.rem(x + d, 4)
        xcopies.append(
            send(act.at[to], ybuf.at[y, x], xs.at[d - 1], xr.at[d - 1], at(y, to), col)
        )
    ybuf[y, x] = act[x]
    kvcopy.wait()
    untangle((2, 3))
    launch(2)
    for copy in xcopies:
        copy.wait_recv()
    yring = Ring(
        y,
        lambda o: (at(o, x), col),
        lambda o: ybuf.at[o],
        lambda o, i: ybuf.at[o, pl.ds(2 * i, 2)],
        lambda i: ys.at[i],
        lambda i: yr.at[i],
    )
    yring.start()
    pump(1)
    untangle((5, 6, 7, 8))
    ocopy.wait()
    wo[col] = wraw[...].T
    yring.forward()
    pump(2)
    launch(3)
    yring.finish()
    for s in range(4):
        request = request_of(y * 4 + s)
        abuf[s, col] = ybuf[lax.div(request, 4), lax.rem(request, 4)]
    zring = Ring(
        z,
        lambda o: (row, o * 2 + core),
        lambda o: abuf.at[:, o * 2 + core],
        lambda o, i: abuf.at[pl.ds(2 * i, 2), o * 2 + core],
        lambda i: zs.at[i],
        lambda i: zr.at[i],
    )
    zring.start()
    ccopies = []

    def across(view):
        i = len(ccopies)
        ccopies.append(send(view, view, cs.at[i], cr.at[i], row, other))

    across(zring.block(z))
    launch(4)
    pump(3)
    launch(5)
    zring.forward()
    across(zring.block(lax.rem(z + 3, 4)))
    across(zring.block(lax.rem(z + 1, 4)))
    pump(4)
    launch(6)
    zring.finish()
    across(zring.block(lax.rem(z + 2, 4)))
    oring = Ring(
        z,
        lambda o: (row, o * 2 + core),
        lambda o: wo.at[o * 2 + core],
        lambda o, i: wo.at[o * 2 + core, pl.ds(384 * i, 384)],
        lambda i: os_.at[i],
        lambda i: or_.at[i],
    )
    oring.start()
    ocopies = []

    def across_out(o):
        i, view = len(ocopies), oring.block(o)
        ocopies.append(send(view, view, ocs.at[i], ocr.at[i], row, other))

    for copy in ccopies:
        copy.wait_recv()

    def multiply(part):
        wring[part].finish()

        def block(i, carry):
            to = lax.rem(x + i + 1, 4)
            out = jnp.dot(
                abuf[to].reshape(256, 1792),
                wbuf[part].reshape(1792, WIDE),
                preferred_element_type=F32,
            )
            acc[part] = out

            @pl.when(i < 3)
            def _():
                psend[part, i] = out.astype(BF16)
                send(
                    psend.at[part, i], rbuf.at[part, i], ps.at[part, i], pr.at[part, i],
                    at(y, to), col,
                )

            return carry

        lax.fori_loop(0, 4, block, 0)

    def arrived(part, i):
        return pltpu.make_async_remote_copy(
            src_ref=psend.at[part, i],
            dst_ref=rbuf.at[part, i],
            send_sem=ps.at[part, i],
            recv_sem=pr.at[part, i],
            device_id=(at(y, lax.rem(x + i + 1, 4)), col),
            device_id_type=MESH,
        )

    def total(part):
        for i in range(3):
            arrived(part, i).wait_recv()
        out = acc[part]
        for i in range(3):
            out = out + rbuf[part, i].astype(F32)
        kind, pair = ORDER[part]
        lanes = slice(pair * WIDE, (pair + 1) * WIDE)
        if kind == 0:
            qbuf[pair] = ((out + bq_ref[lanes][None]) * (HEAD**-0.5)).astype(BF16)
        else:
            to_ref = (k_ref, v_ref)[kind - 1]
            to_ref[:, lanes] = (out + bkv_ref[kind - 1 : kind, lanes]).astype(BF16)

    m_s[...] = jnp.full_like(m_s, NEG)
    l_s[...] = jnp.zeros_like(l_s)
    o_s[...] = jnp.zeros_like(o_s)
    length = len_ref[request_of(row)]

    def visit(pair, keys, values, bias):
        for j in range(2):
            h = pair * 2 + j
            lanes = slice(j * HEAD, (j + 1) * HEAD)
            scores = lax.dot_general(
                qbuf[pair, :, lanes], keys[:, lanes], (((1,), (1,)), ((), ())),
                preferred_element_type=F32,
            )
            scores = scores + bias
            old = m_s[h]
            new = jnp.maximum(old, jnp.max(scores, axis=1, keepdims=True))
            probs = jnp.exp(scores - new)
            factor = jnp.exp(old - new)
            m_s[h] = new
            l_s[h] = l_s[h] * factor + jnp.sum(probs, axis=1, keepdims=True)
            o_s[h] = o_s[h] * factor + jnp.dot(
                probs.astype(BF16), values[:, lanes], preferred_element_type=F32
            )

    def cached(pair, begin, end):
        def step(block, carry):
            n = pair * BLOCKS + block
            slot = lax.rem(n, 2)
            for copy in fetch(n):
                copy.wait()

            @pl.when(n + 1 < 3 * BLOCKS)
            def _():
                for copy in fetch(n + 1):
                    copy.start()

            pos = block * KEYS + lax.broadcasted_iota(jnp.int32, (1, KEYS), 1)
            visit(pair, kbuf[slot], vbuf[slot], jnp.where(pos < length, 0.0, NEG))
            return carry

        lax.fori_loop(begin, end, step, 0)

    late = lax.broadcasted_iota(jnp.int32, (256, 256), 1) > lax.broadcasted_iota(
        jnp.int32, (256, 256), 0
    )
    causal = jnp.where(late, NEG, 0.0)

    def fresh(pair):
        lanes = slice(pair * WIDE, (pair + 1) * WIDE)
        visit(pair, k_ref[:, lanes], v_ref[:, lanes], causal)
        for j in range(2):
            h = pair * 2 + j
            done = (o_s[h] / l_s[h]).astype(BF16)
            asend[pair, :, :, :, j * HEAD : (j + 1) * HEAD] = done.reshape(8, 2, 16, HEAD)

    ag = (ag0, ag1, ag2)
    hcopies = [[], [], []]

    def share(pair):
        mine = ag[pair]
        for d in range(1, 8):
            to = lax.rem(col + d, 8)
            hcopies[pair].append(
                send(asend.at[pair, to], mine.at[:, y, x, col], hs.at[pair, d - 1], hr.at[pair, d - 1],
                     row, to)
            )
        mine[:, y, x, col] = asend[pair, col]

    xline = lambda o: (at(y, o), col)
    yline = lambda o: (at(o, x), col)

    def rings(pair):
        mine = ag[pair]

        def sems(phase, k):
            return (lambda i: gs.at[pair, phase, k, i]), (lambda i: gr.at[pair, phase, k, i])

        if pair < HEAVY:
            return (
                [Ring(y, yline, lambda o: mine.at[:, o, x], lambda o, i: mine.at[i, o, x], *sems(0, 0))],
                [Ring(x, xline, lambda o: mine.at[:, :, o], lambda o, i: mine.at[i, :, o], *sems(1, 0))],
            )
        return (
            [
                Ring(x, xline, lambda o: mine.at[0, y, o],
                     lambda o, i: mine.at[0, y, o, pl.ds(4 * i, 4)], *sems(0, 0)),
                Ring(y, yline, lambda o: mine.at[1, o, x],
                     lambda o, i: mine.at[1, o, x, pl.ds(4 * i, 4)], *sems(0, 1)),
            ],
            [
                Ring(y, yline, lambda o: mine.at[0, o],
                     lambda o, i: mine.at[0, o, pl.ds(2 * i, 2)], *sems(1, 0)),
                Ring(x, xline, lambda o: mine.at[1, :, o],
                     lambda o, i: mine.at[1, pl.ds(2 * i, 2), o], *sems(1, 1)),
            ],
        )

    gather = [rings(pair) for pair in range(3)]

    def stage(pair, number):
        first, second = gather[pair]
        if number == 0:
            for copy in hcopies[pair]:
                copy.wait_recv()
            for ring in first:
                ring.start()
        elif number == 1:
            for ring in first:
                ring.forward()
        elif number == 2:
            for ring in first:
                ring.finish()
            for ring in second:
                ring.start()
        elif number == 3:
            for ring in second:
                ring.forward()
        else:
            for ring in second:
                ring.finish()

    home = lax.div(row, 2)
    which = lax.rem(row, 2)

    def last(q):
        return pltpu.make_async_remote_copy(
            src_ref=fsend.at[q],
            dst_ref=frecv.at[which, col],
            send_sem=fs.at[q],
            recv_sem=fr.at[which, col],
            device_id=(q, home),
            device_id_type=MESH,
        )

    def stays(q):
        return jnp.logical_and(q == row, home == col)

    def hand(q, carry):
        fsend[q] = oacc[pl.ds(pl.multiple_of(q * 32, 32), 32), :].astype(BF16)

        @pl.when(jnp.logical_not(stays(q)))
        def _():
            last(q).start()

        @pl.when(stays(q))
        def _():
            frecv[which, col] = fsend[q]

        return carry

    def output(pair):
        mine = ag[pair]

        def pick(q, carry):
            owner = owner_ref[q]
            for h in range(2):
                rows = mine[h, lax.div(owner, 4), lax.rem(owner, 4)]
                for c in range(8):
                    lhs[pl.ds(pl.multiple_of(q * 32 + h * 16, 16), 16), c * WIDE : (c + 1) * WIDE] = rows[c]
            return carry

        lax.fori_loop(0, 16, pick, 0)

        def block(i, carry):
            rows = pl.ds(pl.multiple_of(i * 256, 256), 256)
            out = jnp.dot(
                lhs[rows, :],
                wo[:, pair * WIDE : (pair + 1) * WIDE, :].reshape(8 * WIDE, 448),
                preferred_element_type=F32,
            )
            oacc[rows, :] = out if pair == 0 else oacc[rows, :] + out
            return lax.fori_loop(i * 8, i * 8 + 8, hand, carry) if pair == 2 else carry

        lax.fori_loop(0, 2, block, 0)

    multiply(0)
    pump(5)
    multiply(1)
    multiply(2)
    launch(7)
    total(0)
    cached(0, 0, BLOCKS // 2)
    pump(6)
    launch(8)
    multiply(3)
    oring.forward()
    across_out(z)
    across_out(lax.rem(z + 3, 4))
    across_out(lax.rem(z + 1, 4))
    cached(0, BLOCKS // 2, BLOCKS)
    pump(7)
    multiply(4)
    total(2)
    total(3)
    fresh(0)
    share(0)
    total(1)
    cached(1, 0, BLOCKS // 2)
    pump(8)
    multiply(5)
    cached(1, BLOCKS // 2, BLOCKS)
    multiply(6)
    oring.finish()
    across_out(lax.rem(z + 2, 4))
    total(4)
    cached(2, 0, BLOCKS // 2)
    multiply(7)
    total(5)
    total(6)
    fresh(1)
    share(1)
    multiply(8)
    stage(0, 0)
    stage(1, 0)
    cached(2, BLOCKS // 2, BLOCKS)
    stage(0, 1)
    stage(1, 1)
    total(7)
    stage(0, 2)
    total(8)
    fresh(2)
    share(2)
    stage(1, 2)
    stage(0, 3)
    stage(2, 0)
    stage(2, 1)
    for copy in ocopies:
        copy.wait_recv()
    stage(1, 3)
    stage(2, 2)
    stage(0, 4)
    output(0)
    stage(1, 4)
    output(1)
    stage(2, 3)
    stage(2, 4)
    output(2)

    rcopy.wait()
    for k in range(2):
        for c in range(8):

            @pl.when(jnp.logical_not(jnp.logical_and(2 * col + k == row, col == c)))
            def _():
                pltpu.make_async_remote_copy(
                    src_ref=fsend.at[0], dst_ref=frecv.at[k, c], send_sem=fs.at[0],
                    recv_sem=fr.at[k, c], device_id=(2 * col + k, c), device_id_type=MESH,
                ).wait_recv()

        lanes = slice(k * 448, (k + 1) * 448)
        out_ref[:, lanes] = (
            frecv[k].reshape(256, 448).astype(F32) + bo_ref[lanes][None] + res[...][:, lanes].astype(F32)
        ).astype(BF16)

    def sent(q, carry):
        @pl.when(jnp.logical_not(stays(q)))
        def _():
            last(q).wait_send()

        return carry

    lax.fori_loop(0, 16, sent, 0)
    for copy in xcopies + ccopies + ocopies + sum(hcopies, []):
        copy.wait_send()
    for ring in [yring, zring, oring] + wring + [r for g in gather for rs in g for r in rs]:
        ring.drain()
    for part in range(PARTS):
        for i in range(3):
            arrived(part, i).wait_send()


def layer(owner_slot, lengths, hidden, gain, shift, wq, wkv, bq, bkv, cache_k, cache_v, w_out, bo):
    dma = pltpu.SemaphoreType.DMA
    vmem = pl.BlockSpec(memory_space=pltpu.VMEM)
    smem = pl.BlockSpec(memory_space=pltpu.SMEM)
    hbm = pl.BlockSpec(memory_space=pl.ANY)
    out = jax.ShapeDtypeStruct((256, 768), BF16)
    return pl.pallas_call(
        layer_kernel,
        out_shape=(jax.ShapeDtypeStruct((256, 896), BF16), out, out),
        in_specs=[smem, smem, hbm, vmem, vmem, hbm, hbm, vmem, vmem, hbm, hbm, hbm, vmem],
        out_specs=(vmem, vmem, vmem),
        scratch_shapes=[
            pltpu.VMEM((32, 7168), BF16),
            pltpu.VMEM((4, 32, 1792), BF16),
            pltpu.VMEM((4, 4, 32, 1792), BF16),
            pltpu.VMEM((4, 8, 32, 1792), BF16),
            pltpu.VMEM((PARTS, 4, 448, WIDE), BF16),
            pltpu.VMEM((PARTS, 3, 256, WIDE), BF16),
            pltpu.VMEM((PARTS, 3, 256, WIDE), BF16),
            pltpu.VMEM((PARTS, 256, WIDE), F32),
            pltpu.VMEM((3, 256, WIDE), BF16),
            pltpu.VMEM((2, KEYS, WIDE), BF16),
            pltpu.VMEM((2, KEYS, WIDE), BF16),
            pltpu.VMEM((6, 256, 1), F32),
            pltpu.VMEM((6, 256, 1), F32),
            pltpu.VMEM((6, 256, HEAD), F32),
            pltpu.VMEM((3, 8, 2, 16, WIDE), BF16),
            pltpu.VMEM((2, 4, 4, 8, 16, WIDE), BF16),
            pltpu.VMEM((2, 4, 4, 8, 16, WIDE), BF16),
            pltpu.VMEM((2, 4, 4, 8, 16, WIDE), BF16),
            pltpu.VMEM((8, 768, 448), BF16),
            pltpu.VMEM((512, 8 * WIDE), BF16),
            pltpu.VMEM((512, 448), F32),
            pltpu.VMEM((16, 32, 448), BF16),
            pltpu.VMEM((2, 8, 32, 448), BF16),
            pltpu.VMEM((256, 896), BF16),
            pltpu.VMEM((448, 768), BF16),
            pltpu.VMEM((448, 2, 768), BF16),
            dma,
            dma((PARTS,)),
            dma((2,)), dma((2,)),
            dma((3,)), dma((3,)),
            dma((4,)), dma((4,)),
            dma((4,)), dma((4,)),
            dma((4,)), dma((4,)),
            dma((PARTS, 4)), dma((PARTS, 4)),
            dma((PARTS, 3)), dma((PARTS, 3)),
            dma, dma,
            dma((4,)), dma((4,)),
            dma((4,)), dma((4,)),
            dma((3, 7)), dma((3, 7)),
            dma((3, 2, 2, 4)), dma((3, 2, 2, 4)),
            dma((16,)), dma((2, 8)),
        ],
        compiler_params=pltpu.CompilerParams(
            collective_id=0, has_side_effects=True, vmem_limit_bytes=58 * 2**20
        ),
        name="layer",
    )(owner_slot, lengths, hidden, gain, shift, wq, wkv, bq, bkv, cache_k, cache_v, w_out, bo)


def settle_kernel(a_ref, b_ref, c_ref, a_out, b_out, c_out):
    a_out[...] = a_ref[...]
    b_out[...] = b_ref[...]
    c_out[...] = c_ref[...]


def settle(*arrays):
    def half(a):
        return pl.BlockSpec((a.shape[0] // 2, a.shape[1]), lambda i: (i, 0))

    return pl.pallas_call(
        settle_kernel,
        out_shape=tuple(jax.ShapeDtypeStruct(a.shape, a.dtype) for a in arrays),
        grid=(2,),
        in_specs=[half(a) for a in arrays],
        out_specs=tuple(half(a) for a in arrays),
        name="settle",
    )(*arrays)


def local(
    hidden_in, norm_gain, norm_bias, w_query, w_keyval, bias_query, bias_keyval,
    cache_keys, cache_values, cache_lengths, owner_slot, w_out, bias_out,
):
    hidden_out, new_k, new_v = layer(
        owner_slot, cache_lengths, hidden_in, norm_gain, norm_bias,
        w_query, w_keyval, bias_query, bias_keyval,
        cache_keys[0], cache_values[0], w_out.T, bias_out,
    )
    hidden_out, new_k, new_v = settle(hidden_out, new_k, new_v)
    return (hidden_out, new_k[None], new_v[None])


def solution(mesh):
    placed = (
        P("row", None), P(), P(), P("row", "col"), P("row", None, "col"), P("col"), P(None, "col"),
        P("row", None, "col"), P("row", None, "col"), P(), P(), P("col", "row"), P("col"),
    )
    return jax.shard_map(
        local,
        mesh=mesh,
        in_specs=placed,
        out_specs=(P("row", "col"), P("row", None, "col"), P("row", None, "col")),
        check_vma=False,
    )
```
